512 devices in a mesh: feat: 16 (over z), img: 32 (over x, y, core).
Axes of the slice: x: 4, y: 4, z: 16, core: 2. Of those that a mesh axis runs over, the one named last changes fastest.
Arguments:
- features: bfloat16 [1792, 61440], P('img', 'feat'), may hold values from -6 to 6
- proj_in: bfloat16 [61440, 768], P('feat', 'img'), may hold values from -0.0234375 to 0.0234375
- proj_out: bfloat16 [768, 512], P('feat'), may hold values from -0.21875 to 0.21875
- centres: bfloat16 [262144, 512], P(('feat', 'img')), may hold values from -0.25 to 0.25
- labels: int32 [1792], P('img'), may hold values from 0 to 262143
Outputs:
- centre_grad: float32 [262144, 512], P(('feat', 'img'))
- emb_grad: float32 [1792, 512], P('img', 'feat')
The draws below stay inside these ranges and needn't reach their ends.
Inputs may be any that keep to these rules, and one draw needn't show every extreme that they name: `labels`: each image's identity is among the sampled centres, at this position.
All inputs are finite; a program needn't handle non-finite values.
Results may differ from the reference program's by a relative error of at most 0.006.
Values may be sent and summed in bfloat16 or wider, within the bound.
No kernel may reach another device: no remote copies, remote signals or barrier semaphores. Data moves between devices by JAX's collectives and lax.ppermute only.
A program may use at most 64 MiB of HBM per device.

```python
import jax
import jax.numpy as jnp
from jax import lax

FEATS = 61440
HID = 768
EMB = 512
CEN_DEV = 512
IMAGES = 1792
CENTRES = 262144
N_FEAT = 16
N_IMG = 32


def plant(entries, stream_key, least, high):
    extent = entries.shape
    spot = [jax.random.randint(jax.random.fold_in(stream_key, axis), (), 0, extent[axis]) for axis in range(len(extent))]
    entries = entries.at[tuple(spot)].set(least)
    longest = extent.index(max(extent))
    spot[longest] = (spot[longest] + 1) % extent[longest]
    return entries.at[tuple(spot)].set(high)


def level_of(key, extent, split, least, largest):
    level, own = 1.0, jax.random.fold_in(key, 6)
    for dim, shards_of in split:
        steps = jnp.exp(jax.random.uniform(jax.random.fold_in(own, dim), (shards_of,), jnp.float32, least / len(split), largest / len(split)))
        level = level * jnp.repeat(steps, extent[dim] // shards_of).reshape([-1 if axis == dim else 1 for axis in range(len(extent))])
    return level


def bell_draw(stream_key, extent, spread, limit, pieces=(), kind=jnp.bfloat16):
    result = jax.random.normal(stream_key, extent, jnp.float32) * spread
    if len(pieces) > 0:
        result = level_of(stream_key, extent, pieces, -0.22, 0.18) * result
    return jnp.clip(result, min=-limit, max=limit).astype(kind)


def setup_inputs(seed: int = 0) -> dict:
    key_of = jax.random.split(jax.random.key(seed), 6)
    return {
        "features": bell_draw(key_of[0], (IMAGES, FEATS), 1.0, 6.0, ((0, 32), (1, 16))),
        "proj_in": bell_draw(key_of[1], (FEATS, HID), FEATS ** -0.5, 0.0234375, ((0, 16), (1, 32))),
        "proj_out": bell_draw(key_of[2], (HID, EMB), HID ** -0.5, 0.21875, ((0, 16),)),
        "centres": bell_draw(key_of[3], (CENTRES, EMB), EMB ** -0.5, 0.25, ((0, 512),)),
        "labels": plant(jax.random.randint(key_of[4], (IMAGES,), 0, CENTRES), jax.random.fold_in(key_of[4], 1), 0, CENTRES - 1).astype(jnp.int32),
    }


norm_eps = 1e-06
scale_logit = 64.0
margin_angle = 0.5
sine_floor = 0.04

def reference(features, proj_in, proj_out, centres, labels):
    hidden = jnp.dot(features, proj_in, preferred_element_type=jnp.float32).astype(jnp.bfloat16)
    embed = jnp.dot(hidden, proj_out, preferred_element_type=jnp.float32)
    inverse = lax.rsqrt(lax.optimization_barrier(jnp.sum(embed * embed, axis=1)) + norm_eps)
    unit = embed * inverse[:, None]
    unit_low = unit.astype(jnp.bfloat16)
    count = N_FEAT * N_IMG
    blocks = centres.reshape(count, CEN_DEV, EMB)
    starts = jnp.arange(count, dtype=jnp.int32) * CEN_DEV
    cos_m = jnp.cos(jnp.float32(margin_angle))
    sin_m = jnp.sin(jnp.float32(margin_angle))

    def logits(block, begin):
        wide = block.astype(jnp.float32)
        cinv = lax.rsqrt(lax.optimization_barrier(jnp.sum(wide * wide, axis=1)) + norm_eps)
        unit_centre = wide * cinv[:, None]
        centre_low = unit_centre.astype(jnp.bfloat16)
        cosine = jnp.dot(unit_low, centre_low.T, preferred_element_type=jnp.float32)
        position = begin + jnp.arange(CEN_DEV, dtype=jnp.int32)
        target = labels[:, None] == position[None, :]
        inner = 1.0 - cosine * cosine
        sine = jnp.sqrt(jnp.maximum(inner, sine_floor))
        logit = jnp.where(target, scale_logit * (cosine * cos_m - sine * sin_m), scale_logit * cosine)
        return (cosine, target, inner, sine, jnp.exp(logit), cinv, unit_centre, centre_low)

    def totals(pair):
        return lax.optimization_barrier(jnp.sum(logits(pair[0], pair[1])[4], axis=1))
    total = lax.optimization_barrier(jnp.sum(lax.map(totals, (blocks, starts)), axis=0))

    def backward(carry, pair):
        cosine, target, inner, sine, exps, cinv, unit_centre, centre_low = logits(pair[0], pair[1])
        dlogit = exps / total[:, None] - target.astype(jnp.float32)
        slope = cos_m + jnp.where(inner > sine_floor, sin_m * cosine / sine, 0.0)
        dcos = (dlogit * scale_logit * jnp.where(target, slope, 1.0)).astype(jnp.bfloat16)
        gunit = jnp.dot(dcos.T, unit_low, preferred_element_type=jnp.float32)
        grad = cinv[:, None] * (gunit - unit_centre * lax.optimization_barrier(jnp.sum(unit_centre * gunit, axis=1, keepdims=True)))
        carry = carry + jnp.dot(dcos, centre_low, preferred_element_type=jnp.float32)
        return (carry, grad)
    dunit, grads = lax.scan(backward, jnp.zeros((IMAGES, EMB), jnp.float32), (blocks, starts))
    centre_grad = grads.reshape(CENTRES, EMB)
    emb_grad = inverse[:, None] * (dunit - unit * lax.optimization_barrier(jnp.sum(unit * dunit, axis=1, keepdims=True)))
    return (centre_grad, emb_grad)
```

```python
import jax
import jax.numpy as jnp
import numpy as np
from jax import lax
from jax.sharding import Mesh, PartitionSpec as P

norm_eps = 1e-06
scale_logit = 64.0
margin_angle = 0.5
sine_floor = 0.04

NZ, NX, NY, NC = 16, 4, 4, 2
XY = ("x", "y")
SWAP = [(0, 1), (1, 0)]
f32 = jnp.float32
bf16 = jnp.bfloat16


def exchange(blocks, axis):
    return lax.all_to_all(blocks, axis, 0, 0)


def spread(block, axis, count):
    return exchange(jnp.broadcast_to(block[None], (count,) + block.shape), axis)


def partner(block):
    return lax.ppermute(block, "c", SWAP)


def exact_dot(left, right):
    return jnp.dot(left, right.astype(f32), precision=lax.Precision.HIGHEST, preferred_element_type=f32)


def per_device(features, proj_in, proj_out, centres, labels):
    rows, feats = features.shape
    cols = proj_in.shape[1]
    emb = proj_out.shape[1]
    cen = centres.shape[0]
    images = NX * NY * rows
    zi, xi, yi, ci = (lax.axis_index(a) for a in ("z", "x", "y", "c"))

    wide_rows = spread(features, "x", NX).reshape(NX * rows, feats)
    own_cols = spread(proj_in.T, "y", NY).reshape(NY * cols, feats)
    other_cols = partner(own_cols)
    out_rows = spread(proj_out, "z", NZ)
    out_rows = lax.dynamic_slice_in_dim(out_rows, NX * xi, NX, 0)
    own_out = lax.dynamic_slice_in_dim(out_rows, cols * ci, cols, 1).reshape(NY * cols, emb)
    other_out = lax.dynamic_slice_in_dim(out_rows, cols * (1 - ci), cols, 1).reshape(NY * cols, emb)

    all_labels = spread(labels, XY, NX * NY).reshape(images, 1)
    wide = centres.astype(f32)
    cinv = lax.rsqrt(jnp.sum(wide * wide, axis=1) + norm_eps)
    unit_centre = wide * cinv[:, None]
    own_low = unit_centre.astype(bf16)
    low = jnp.concatenate([own_low, partner(own_low)], axis=0)
    seat = ((zi * NX + xi) * NY + yi) * NC
    step = jnp.arange(cen, dtype=jnp.int32)
    position = jnp.concatenate([(seat + ci) * cen + step, (seat + 1 - ci) * cen + step])
    target = all_labels == position[None, :]

    def times(weights, cols_of):
        return lax.dot_general(weights, cols_of, (((1,), (1,)), ((), ())), preferred_element_type=f32)

    part = exact_dot(times(wide_rows, own_cols), own_out) + exact_dot(times(wide_rows, other_cols), other_out)
    part = jnp.sum(exchange(part.reshape(NX, rows, emb), "x"), axis=0)
    lanes = emb // 4
    piece = part.reshape(rows, 4, lanes).transpose(1, 0, 2).reshape(NZ, rows // 4, lanes)
    piece = jnp.sum(exchange(piece, "z"), axis=0)
    embed = spread(piece, "z", NZ).reshape(4, rows, lanes).transpose(1, 0, 2).reshape(rows, emb)
    inverse = lax.rsqrt(jnp.sum(embed * embed, axis=1) + norm_eps)
    unit = embed * inverse[:, None]
    units = spread(unit.astype(bf16), XY, NX * NY).reshape(images, emb)

    chosen = jnp.dot(target.astype(bf16), low, preferred_element_type=f32).astype(bf16)
    chosen = jnp.sum(exchange(chosen.reshape(NX * NY, rows, emb), XY).astype(f32), axis=0)

    cos_m = jnp.cos(f32(margin_angle))
    sin_m = jnp.sin(f32(margin_angle))
    cosine = lax.dot_general(units, low, (((1,), (1,)), ((), ())), preferred_element_type=f32)
    inner = 1.0 - cosine * cosine
    sine = jnp.sqrt(jnp.maximum(inner, sine_floor))
    logit = jnp.where(target, scale_logit * (cosine * cos_m - sine * sin_m), scale_logit * cosine)
    exps = jnp.exp(logit)
    slope = cos_m + jnp.where(inner > sine_floor, sin_m * cosine / sine, 0.0)
    rest = jnp.where(target, 0.0, exps)
    rest_sum = jnp.sum(rest, axis=1)
    rest_cos = jnp.sum(rest * cosine, axis=1)
    hit = jnp.sum(jnp.where(target, exps, 0.0), axis=1)
    hit_slope = jnp.sum(jnp.where(target, slope, 0.0), axis=1)
    hit_turn = jnp.sum(jnp.where(target, slope * cosine, 0.0), axis=1)

    sums = jnp.stack([rest_sum, hit, rest_cos, hit_slope, hit_turn], axis=1)
    owned = sums.reshape(NX * NY, rows, 5).transpose(0, 2, 1)
    owned = jnp.pad(owned, ((0, 0), (0, 3), (0, 128 - rows)))
    totals = jnp.pad((rest_sum + hit).reshape(images // 128, 128), ((0, 8 - images // 128), (0, 0)))
    pack = jnp.concatenate([jnp.broadcast_to(totals[None], (NX * NY, 8, 128)), owned], axis=1)
    pack = jnp.sum(exchange(pack, XY), axis=0)
    pack = jnp.sum(spread(pack, "z", NZ), axis=0)
    total = pack[: images // 128].reshape(images, 1)
    own_rest, own_hit, own_cos, own_slope, own_turn = (pack[8 + k, :rows] for k in range(5))

    pull = jnp.dot(rest.astype(bf16), low, preferred_element_type=f32).astype(bf16)
    pull = jnp.sum(exchange(pull.reshape(NX * NY, rows, emb), XY).astype(f32), axis=0)
    width = emb // NZ

    def by_column(block):
        block = block.astype(bf16).reshape(4, rows // 4, NZ, width)
        return block.transpose(2, 1, 0, 3).reshape(NZ, rows // 4, 4 * width)

    both = jnp.concatenate([by_column(pull), by_column(chosen)], axis=1)
    both = jnp.sum(exchange(both, "z").astype(f32), axis=0)

    def by_row(block):
        return block.reshape(rows // 4, 4, width).transpose(1, 0, 2).reshape(rows, width)

    pull, chosen = by_row(both[: rows // 4]), by_row(both[rows // 4 :])

    weight = scale_logit * hit_slope[:, None] * (hit[:, None] / total - 1.0)
    dcos = jnp.where(target, weight, scale_logit * (rest / total)).astype(bf16)
    gunit = lax.dot_general(dcos, units, (((0,), (0,)), ((), ())), preferred_element_type=f32)
    gunit = gunit[:cen] + partner(gunit[cen:])
    centre_grad = cinv[:, None] * (gunit - unit_centre * jnp.sum(unit_centre * gunit, axis=1, keepdims=True))

    own_scale = scale_logit / (own_rest + own_hit)
    dunit = own_scale[:, None] * (pull - (own_rest * own_slope)[:, None] * chosen)
    along = own_scale * (own_cos - own_rest * own_turn)
    unit_cols = lax.dynamic_slice_in_dim(unit, zi * width, width, 1)
    emb_grad = inverse[:, None] * (dunit - unit_cols * along[:, None])
    return (centre_grad, emb_grad)


def solution(mesh):
    fine = Mesh(np.asarray(mesh.devices).reshape(NZ, NX, NY, NC), ("z", "x", "y", "c"))
    img = ("x", "y", "c")
    every = ("z", "x", "y", "c")
    return jax.shard_map(
        per_device,
        mesh=fine,
        in_specs=(P(img, "z"), P("z", img), P("z", None), P(every, None), P(img)),
        out_specs=(P(every, None), P(img, "z")),
        check_vma=False,
    )
```

```python
import jax
import jax.numpy as jnp
import numpy as np
from jax import lax
from jax.experimental import pallas as pl
from jax.experimental.pallas import tpu as pltpu
from jax.sharding import Mesh, PartitionSpec as P


norm_eps = 1e-06
scale_logit = 64.0
margin_angle = 0.5
sine_floor = 0.04

NZ, NX, NY, NC = 16, 4, 4, 2
XY = ("x", "y")
SWAP = [(0, 1), (1, 0)]
f32 = jnp.float32
bf16 = jnp.bfloat16


def exchange(blocks, axis):
    return lax.all_to_all(blocks, axis, 0, 0)


def spread(block, axis, count):
    return exchange(jnp.broadcast_to(block[None], (count,) + block.shape), axis)


def partner(block):
    return lax.ppermute(block, "c", SWAP)


def shift(block, axis, by):
    return lax.ppermute(block, axis, [(i, (i + by) % 4) for i in range(4)])


def hidden_kernel(seat, mine, left, right, far_a, far_b, own_cols, other_cols, out):
    x, y, c = seat[0], seat[1], seat[2]
    rows = mine.shape[0]
    cols = own_cols.shape[0] // NY
    far = jnp.concatenate([far_a[...], far_b[...]], axis=0)
    zero = jnp.zeros((NY * cols, 64 - rows), f32)

    def times(weights, block):
        return lax.dot_general(weights, block, (((1,), (1,)), ((), ())), preferred_element_type=f32)

    for off, block in ((0, mine[...]), (3, left[...]), (1, right[...]), (2, far)):
        own, other = times(own_cols[...], block), times(other_cols[...], block)
        first, second = jnp.where(c == 0, own, other), jnp.where(c == 0, other, own)
        both = jnp.concatenate([first, zero, second, zero], axis=1)
        for k, y_off in enumerate((0, 3, 1, 2)):
            out[lax.rem(x + off, NX), lax.rem(y + y_off, NY)] = both[k * cols : (k + 1) * cols]


def partial_hidden(seat, blocks, own_cols, other_cols, cols):
    vmem = pl.BlockSpec(memory_space=pltpu.VMEM)
    return pl.pallas_call(
        hidden_kernel,
        out_shape=jax.ShapeDtypeStruct((NX, NY, cols, 128), f32),
        in_specs=[pl.BlockSpec(memory_space=pltpu.SMEM)] + [vmem] * 7,
        out_specs=vmem,
        cost_estimate=pl.CostEstimate(flops=330_000_000, bytes_accessed=3_400_000, transcendentals=0),
    )(seat, *blocks, own_cols, other_cols)


def centre_kernel(centres, own, received, out):
    wide = centres[...].astype(f32)
    cinv = lax.rsqrt(jnp.sum(wide * wide, axis=1, keepdims=True) + norm_eps)
    unit_centre = wide * cinv
    gunit = own[...] + received[...]
    out[...] = cinv * (gunit - unit_centre * jnp.sum(unit_centre * gunit, axis=1, keepdims=True))


def centre_gradient(centres, own, received):
    rows, emb = centres.shape
    block = pl.BlockSpec((rows // 4, emb), lambda i: (i, 0))
    return pl.pallas_call(
        centre_kernel,
        out_shape=jax.ShapeDtypeStruct((rows, emb), f32),
        grid=(4,),
        in_specs=[block] * 3,
        out_specs=block,
        cost_estimate=pl.CostEstimate(flops=3_000_000, bytes_accessed=3_700_000, transcendentals=512),
    )(centres, own, received)


def split_pair(value):
    high = lax.reduce_precision(value, 8, 7)
    return high.astype(bf16), (value - high).astype(bf16)


def step_of(features, proj_in, proj_out, centres, labels):
    rows, _ = features.shape
    cols = proj_in.shape[1]
    emb = proj_out.shape[1]
    cen = centres.shape[0]
    images = NX * NY * rows
    lanes = emb // 4
    zi, xi, yi, ci = (lax.axis_index(a) for a in ("z", "x", "y", "c"))

    out_part = lax.dynamic_slice_in_dim(proj_out, yi * lanes, lanes, 1)
    out_part = spread(out_part, "z", NZ).reshape(NZ * proj_out.shape[0], lanes)
    from_left = shift(features, "x", 1)
    from_right = shift(features, "x", 3)
    cols_in = proj_in.T
    own_cols = [cols_in]
    for by in (1, 3, 2):
        own_cols.append(shift(cols_in, "y", by))
    own_cols = jnp.concatenate(own_cols, axis=0)
    far_a = shift(from_left[:32], "x", 1)
    far_b = shift(from_right[32:], "x", 3)
    other_cols = partner(own_cols)
    seat = jnp.stack([xi, yi, ci]).astype(jnp.int32)
    part = partial_hidden(seat, (features, from_left, from_right, far_a, far_b), own_cols, other_cols, cols)

    all_labels = spread(labels, XY, NX * NY).reshape(images, 1)
    wide = centres.astype(f32)
    cinv = lax.rsqrt(jnp.sum(wide * wide, axis=1) + norm_eps)
    unit_centre = wide * cinv[:, None]
    own_low = unit_centre.astype(bf16)
    low = jnp.concatenate([own_low, partner(own_low)], axis=0)
    chip = ((zi * NX + xi) * NY + yi) * NC
    step = jnp.arange(cen, dtype=jnp.int32)
    position = jnp.concatenate([(chip + ci) * cen + step, (chip + 1 - ci) * cen + step])
    target = all_labels == position[None, :]

    part = exchange(part, "x").reshape(NZ, cols, 128)
    hidden = jnp.sum(exchange(part, "z"), axis=0).astype(bf16)
    hidden = spread(hidden, "z", NZ).reshape(NZ * cols, 128)
    whole = jnp.stack([out_part, shift(out_part, "y", 1), shift(out_part, "y", 3), shift(out_part, "y", 2)])
    order = jnp.stack([lax.rem(yi * 0 + k + 4 - yi, 4) for k in range(4)])
    order = jnp.where(order == 3, 1, jnp.where(order == 1, 2, jnp.where(order == 2, 3, 0)))
    whole = jnp.take(whole, order, axis=0).transpose(1, 0, 2).reshape(NZ, NC, cols, emb)

    def over_rows(left, right):
        return lax.dot_general(left, right, (((0,), (0,)), ((), ())), preferred_element_type=f32)

    embed = over_rows(hidden[:, :rows], whole[:, 0].reshape(NZ * cols, emb))
    embed = embed + over_rows(hidden[:, 64 : 64 + rows], whole[:, 1].reshape(NZ * cols, emb))
    inverse = lax.rsqrt(jnp.sum(embed * embed, axis=1) + norm_eps)
    unit = embed * inverse[:, None]
    units = spread(unit.astype(bf16), XY, NX * NY).reshape(images, emb)

    chosen = jnp.dot(target.astype(bf16), low, preferred_element_type=f32).astype(bf16)
    chosen, units = lax.optimization_barrier((chosen, units))
    chosen = exchange(chosen.reshape(NX * NY, rows, emb), XY)
    chosen = jnp.sum(chosen.astype(f32), axis=0)

    cos_m = jnp.cos(f32(margin_angle))
    sin_m = jnp.sin(f32(margin_angle))
    cosine = lax.dot_general(units, low, (((1,), (1,)), ((), ())), preferred_element_type=f32)
    inner = 1.0 - cosine * cosine
    sine = jnp.sqrt(jnp.maximum(inner, sine_floor))
    logit = jnp.where(target, scale_logit * (cosine * cos_m - sine * sin_m), scale_logit * cosine)
    exps = jnp.exp(logit)
    slope = cos_m + jnp.where(inner > sine_floor, sin_m * cosine / sine, 0.0)
    rest = jnp.where(target, 0.0, exps)
    rest_sum = jnp.sum(rest, axis=1)
    rest_cos = jnp.sum(rest * cosine, axis=1)
    hit = jnp.sum(jnp.where(target, exps, 0.0), axis=1)
    hit_slope = jnp.sum(jnp.where(target, slope, 0.0), axis=1)
    hit_turn = jnp.sum(jnp.where(target, slope * cosine, 0.0), axis=1)

    pull = jnp.dot(rest.astype(bf16), low, preferred_element_type=f32).astype(bf16)
    pull = exchange(pull.reshape(NX * NY, rows, emb), XY)

    sums = jnp.stack([rest_sum, hit, rest_cos, hit_slope, hit_turn]).reshape(5, images // 128, 128)
    sums = lax.psum(lax.psum(sums, "x"), "y").reshape(5, images)
    owned = lax.dynamic_slice_in_dim(sums, (xi * NY + yi) * rows, rows, 1)
    owned = jnp.pad(owned, ((0, 0), (0, 128 - rows)))
    totals = (sums[0] + sums[1]).reshape(images // 128, 128)

    width = emb // NZ

    def by_column(block):
        block = block.astype(bf16).reshape(4, rows // 4, NZ, width)
        return block.transpose(2, 1, 0, 3).reshape(NZ, rows // 4, 4 * width)

    pull = jnp.sum(pull.astype(f32), axis=0)
    common = jnp.concatenate(split_pair(totals) + split_pair(owned), axis=0)
    common = jnp.broadcast_to(common[None], (NZ,) + common.shape)
    pack = jnp.concatenate([by_column(pull), by_column(chosen), common], axis=1)
    pack = exchange(pack, "z")
    pack = jnp.sum(pack.astype(f32), axis=0)

    def by_row(block):
        return block.reshape(rows // 4, 4, width).transpose(1, 0, 2).reshape(rows, width)

    quarter, tall = rows // 4, images // 128
    pull, chosen = by_row(pack[:quarter]), by_row(pack[quarter : 2 * quarter])
    common = pack[2 * quarter :]
    total = (common[:tall] + common[tall : 2 * tall]).reshape(images, 1)
    owned = common[2 * tall : 2 * tall + 5, :rows] + common[2 * tall + 5 :, :rows]
    own_rest, own_hit, own_cos, own_slope, own_turn = (owned[k] for k in range(5))

    cosine_t = lax.dot_general(low, units, (((1,), (1,)), ((), ())), preferred_element_type=f32)
    target_t = position[:, None] == all_labels.reshape(1, images)
    rest_t = jnp.where(target_t, 0.0, jnp.exp(scale_logit * cosine_t)).astype(bf16)
    rest_t, target_t = lax.optimization_barrier((rest_t, target_t.astype(bf16)))
    weight = scale_logit * hit_slope[:, None] * (hit[:, None] / total - 1.0)
    scaled = (units.astype(f32) * (scale_logit / total)).astype(bf16)
    aimed = (units.astype(f32) * weight).astype(bf16)

    def gradient_of(part):
        left = jnp.dot(rest_t[part], scaled, preferred_element_type=f32)
        return left + jnp.dot(target_t[part], aimed, preferred_element_type=f32)

    received = partner(gradient_of(slice(cen, None)))
    centre_grad = centre_gradient(centres, gradient_of(slice(0, cen)), received)

    own_scale = scale_logit / (own_rest + own_hit)
    dunit = own_scale[:, None] * (pull - (own_rest * own_slope)[:, None] * chosen)
    along = own_scale * (own_cos - own_rest * own_turn)
    unit_cols = lax.dynamic_slice_in_dim(unit, zi * width, width, 1)
    emb_grad = inverse[:, None] * (dunit - unit_cols * along[:, None])
    return (centre_grad, emb_grad)


def solution(mesh):
    fine = Mesh(np.asarray(mesh.devices).reshape(NZ, NX, NY, NC), ("z", "x", "y", "c"))
    img = ("x", "y", "c")
    every = ("z", "x", "y", "c")
    return jax.shard_map(
        step_of,
        mesh=fine,
        in_specs=(P(img, "z"), P("z", img), P("z", None), P(every, None), P(img)),
        out_specs=(P(every, None), P(img, "z")),
        check_vma=False,
    )
```

```python
import jax
import jax.numpy as jnp
import numpy as np
from jax import lax
from jax.experimental import pallas as pl
from jax.experimental.pallas import tpu as pltpu
from jax.sharding import Mesh, PartitionSpec as P


norm_eps = 1e-06
scale_logit = 64.0
margin_angle = 0.5
sine_floor = 0.04

NZ, NX, NY, NC = 16, 4, 4, 2
XY = ("x", "y")
SWAP = [(0, 1), (1, 0)]
f32 = jnp.float32
bf16 = jnp.bfloat16


def exchange(blocks, axis):
    return lax.all_to_all(blocks, axis, 0, 0)


def spread(block, axis, count):
    return exchange(jnp.broadcast_to(block[None], (count,) + block.shape), axis)


def partner(block):
    return lax.ppermute(block, "c", SWAP)


def shift(block, axis, by):
    return lax.ppermute(block, axis, [(i, (i + by) % 4) for i in range(4)])


def hidden_kernel(seat, mine, left, right, far, own_cols, other_cols, out, held):
    x, y, c = seat[0], seat[1], seat[2]
    rows, feats = mine.shape
    cols = own_cols.shape[0] // NY
    for k, block in enumerate((mine, left, right, far)):
        held[k, :rows] = block[...]
        held[k, rows:] = jnp.zeros((64 - rows, feats), bf16)
    blocks = held[...].reshape(NX * 64, feats)

    def times(weights):
        return lax.dot_general(weights, blocks, (((1,), (1,)), ((), ())), preferred_element_type=f32)

    own, other = times(own_cols[...]), times(other_cols[...])
    first, second = jnp.where(c == 0, own, other), jnp.where(c == 0, other, own)
    beside = y + 1 - 2 * lax.rem(y, 2)
    for k, off in enumerate((0, 3, 1, 2)):
        both = jnp.concatenate([first[:, 64 * k : 64 * k + 64], second[:, 64 * k : 64 * k + 64]], axis=1)
        for j, at in enumerate((y, beside, 3 - y, 3 - beside)):
            out[lax.rem(x + off, NX), at] = both[j * cols : (j + 1) * cols]


def partial_hidden(seat, blocks, own_cols, other_cols, cols):
    vmem = pl.BlockSpec(memory_space=pltpu.VMEM)
    return pl.pallas_call(
        hidden_kernel,
        out_shape=jax.ShapeDtypeStruct((NX, NY, cols, 128), f32),
        in_specs=[pl.BlockSpec(memory_space=pltpu.SMEM)] + [vmem] * 6,
        out_specs=vmem,
        scratch_shapes=[pltpu.VMEM((NX, 64, blocks[0].shape[1]), bf16)],
        cost_estimate=pl.CostEstimate(flops=330_000_000, bytes_accessed=3_400_000, transcendentals=0),
    )(seat, *blocks, own_cols, other_cols)


def centre_kernel(centres, own, received, out):
    wide = centres[...].astype(f32)
    cinv = lax.rsqrt(jnp.sum(wide * wide, axis=1, keepdims=True) + norm_eps)
    unit_centre = wide * cinv
    gunit = own[...] + received[...]
    out[...] = cinv * (gunit - unit_centre * jnp.sum(unit_centre * gunit, axis=1, keepdims=True))


def centre_gradient(centres, own, received):
    rows, emb = centres.shape
    block = pl.BlockSpec(memory_space=pltpu.VMEM)
    return pl.pallas_call(
        centre_kernel,
        out_shape=jax.ShapeDtypeStruct((rows, emb), f32),
        in_specs=[block] * 3,
        out_specs=block,
        cost_estimate=pl.CostEstimate(flops=3_000_000, bytes_accessed=3_700_000, transcendentals=512),
    )(centres, own, received)


def split_pair(value):
    high = lax.reduce_precision(value, 8, 7)
    return high.astype(bf16), (value - high).astype(bf16)


def step_of(features, proj_in, proj_out, centres, labels):
    rows, _ = features.shape
    cols = proj_in.shape[1]
    emb = proj_out.shape[1]
    cen = centres.shape[0]
    images = NX * NY * rows
    zi, xi, yi, ci = (lax.axis_index(a) for a in ("z", "x", "y", "c"))

    from_left = shift(features, "x", 1)
    from_right = shift(features, "x", 3)
    own_cols = proj_in.T
    own_cols = jnp.concatenate([own_cols, lax.ppermute(own_cols, "y", [(0, 1), (1, 0), (2, 3), (3, 2)])], axis=0)
    own_cols = jnp.concatenate([own_cols, lax.ppermute(own_cols, "y", [(0, 3), (3, 0), (1, 2), (2, 1)])], axis=0)
    from_far = shift(from_left, "x", 1)
    whole = spread(proj_out, "z", NZ)
    other_cols = partner(own_cols)
    seat = jnp.stack([xi, yi, ci]).astype(jnp.int32)
    part = partial_hidden(seat, (features, from_left, from_right, from_far), own_cols, other_cols, cols)
    part = exchange(part, "x").reshape(NZ, cols, 128)

    part, labels = lax.optimization_barrier((part, labels))
    all_labels = lax.dynamic_update_slice_in_dim(jnp.zeros(NY * rows, jnp.int32), labels, yi * rows, 0)
    all_labels = lax.psum(all_labels, "y")
    all_labels = lax.dynamic_update_slice_in_dim(jnp.zeros(images, jnp.int32), all_labels, xi * NY * rows, 0)
    all_labels = lax.psum(all_labels, "x")
    all_labels = all_labels.reshape(images, 1)
    wide = centres.astype(f32)
    cinv = lax.rsqrt(jnp.sum(wide * wide, axis=1) + norm_eps)
    unit_centre = wide * cinv[:, None]
    own_low = unit_centre.astype(bf16)
    low = jnp.concatenate([own_low, partner(own_low)], axis=0)
    chip = ((zi * NX + xi) * NY + yi) * NC
    step = jnp.arange(cen, dtype=jnp.int32)
    position = jnp.concatenate([(chip + ci) * cen + step, (chip + 1 - ci) * cen + step])
    target = all_labels == position[None, :]

    hidden = jnp.sum(exchange(part, "z"), axis=0).astype(bf16)
    hidden = spread(hidden, "z", NZ).reshape(NZ * cols, 128)

    def over_rows(left, right):
        return lax.dot_general(left, right, (((0,), (0,)), ((), ())), preferred_element_type=f32)

    embed = over_rows(hidden[:, :rows], whole[:, :cols].reshape(NZ * cols, emb))
    embed = embed + over_rows(hidden[:, 64 : 64 + rows], whole[:, cols:].reshape(NZ * cols, emb))
    inverse = lax.rsqrt(jnp.sum(embed * embed, axis=1) + norm_eps)
    unit = embed * inverse[:, None]
    units = spread(unit.astype(bf16), XY, NX * NY).reshape(images, emb)

    chosen = jnp.dot(target.astype(bf16), low, preferred_element_type=f32).astype(bf16)
    chosen, units = lax.optimization_barrier((chosen, units))
    chosen = exchange(chosen.reshape(NX * NY, rows, emb), XY)
    chosen = jnp.sum(chosen.astype(f32), axis=0)

    cos_m = jnp.cos(f32(margin_angle))
    sin_m = jnp.sin(f32(margin_angle))
    cosine = lax.dot_general(units, low, (((1,), (1,)), ((), ())), preferred_element_type=f32)
    inner = 1.0 - cosine * cosine
    sine = jnp.sqrt(jnp.maximum(inner, sine_floor))
    logit = jnp.where(target, scale_logit * (cosine * cos_m - sine * sin_m), scale_logit * cosine)
    exps = jnp.exp(logit)
    slope = cos_m + jnp.where(inner > sine_floor, sin_m * cosine / sine, 0.0)
    rest = jnp.where(target, 0.0, exps)
    rest_sum = jnp.sum(rest, axis=1)
    rest_cos = jnp.sum(rest * cosine, axis=1)
    hit = jnp.sum(jnp.where(target, exps, 0.0), axis=1)
    hit_slope = jnp.sum(jnp.where(target, slope, 0.0), axis=1)
    hit_turn = jnp.sum(jnp.where(target, slope * cosine, 0.0), axis=1)

    pull = jnp.dot(rest.astype(bf16), low, preferred_element_type=f32).astype(bf16).reshape(NX * NY, rows, emb)
    tall = images // 128
    totals = jnp.concatenate(split_pair((rest_sum + hit).reshape(tall, 128)), axis=0)
    totals = jnp.pad(totals, ((0, 16 - 2 * tall), (0, 0))).reshape(4, emb)
    totals = jnp.broadcast_to(totals[None], (NX * NY, 4, emb))
    owned = jnp.stack([rest_sum, hit, rest_cos, hit_slope, hit_turn]).reshape(5, NX * NY, rows)
    owned = jnp.pad(owned.transpose(1, 0, 2), ((0, 0), (0, 0), (0, 64 - rows)))
    owned = jnp.concatenate(split_pair(owned), axis=1).reshape(NX * NY, 640)
    owned = jnp.pad(owned, ((0, 0), (0, 4 * emb - 640))).reshape(NX * NY, 4, emb)
    pull = jnp.concatenate([pull, totals, owned], axis=1)
    pull = exchange(pull, XY)
    pull = jnp.sum(pull.astype(f32), axis=0)
    totals = pull[rows : rows + 4].reshape(16, 128)
    totals = totals[:tall] + totals[tall : 2 * tall]
    owned = pull[rows + 4 :].reshape(4 * emb)[:640].reshape(10, 64)
    owned = jnp.pad(owned[:5] + owned[5:], ((0, 0), (0, 64)))

    width = emb // NZ

    def by_column(block):
        block = block.astype(bf16).reshape(4, rows // 4, NZ, width)
        return block.transpose(2, 1, 0, 3).reshape(NZ, rows // 4, 4 * width)

    pull = pull[:rows]
    common = jnp.concatenate(split_pair(totals) + split_pair(owned), axis=0)
    common = jnp.broadcast_to(common[None], (NZ,) + common.shape)
    pack = jnp.concatenate([by_column(pull), by_column(chosen), common], axis=1)
    pack = exchange(pack, "z")
    pack = jnp.sum(pack.astype(f32), axis=0)

    def by_row(block):
        return block.reshape(rows // 4, 4, width).transpose(1, 0, 2).reshape(rows, width)

    quarter = rows // 4
    pull, chosen = by_row(pack[:quarter]), by_row(pack[quarter : 2 * quarter])
    common = pack[2 * quarter :]
    total = (common[:tall] + common[tall : 2 * tall]).reshape(images, 1)
    owned = common[2 * tall : 2 * tall + 5, :rows] + common[2 * tall + 5 :, :rows]
    own_rest, own_hit, own_cos, own_slope, own_turn = (owned[k] for k in range(5))

    cosine_t = lax.dot_general(low, units, (((1,), (1,)), ((), ())), preferred_element_type=f32)
    target_t = position[:, None] == all_labels.reshape(1, images)
    rest_t = jnp.where(target_t, 0.0, jnp.exp(scale_logit * cosine_t)).astype(bf16)
    rest_t, target_t = lax.optimization_barrier((rest_t, target_t.astype(bf16)))
    weight = scale_logit * hit_slope[:, None] * (hit[:, None] / total - 1.0)
    scaled = (units.astype(f32) * (scale_logit / total)).astype(bf16)
    aimed = (units.astype(f32) * weight).astype(bf16)

    def gradient_of(part):
        left = jnp.dot(rest_t[part], scaled, preferred_element_type=f32)
        return left + jnp.dot(target_t[part], aimed, preferred_element_type=f32)

    received = partner(gradient_of(slice(cen, None)))
    centre_grad = centre_gradient(centres, gradient_of(slice(0, cen)), received)

    own_scale = scale_logit / (own_rest + own_hit)
    dunit = own_scale[:, None] * (pull - (own_rest * own_slope)[:, None] * chosen)
    along = own_scale * (own_cos - own_rest * own_turn)
    unit_cols = lax.dynamic_slice_in_dim(unit, zi * width, width, 1)
    emb_grad = inverse[:, None] * (dunit - unit_cols * along[:, None])
    return (centre_grad, emb_grad)


def solution(mesh):
    fine = Mesh(np.asarray(mesh.devices).reshape(NZ, NX, NY, NC), ("z", "x", "y", "c"))
    img = ("x", "y", "c")
    every = ("z", "x", "y", "c")
    return jax.shard_map(
        step_of,
        mesh=fine,
        in_specs=(P(img, "z"), P("z", img), P("z", None), P(every, None), P(img)),
        out_specs=(P(every, None), P(img, "z")),
        check_vma=False,
    )
```

```python
import jax
import jax.numpy as jnp
import numpy as np
from jax import lax
from jax.experimental import pallas as pl
from jax.experimental.pallas import tpu as pltpu
from jax.sharding import Mesh, PartitionSpec as P


norm_eps = 1e-06
scale_logit = 64.0
margin_angle = 0.5
sine_floor = 0.04

NZ, NX, NY, NC = 16, 4, 4, 2
XY = ("x", "y")
SWAP = [(0, 1), (1, 0)]
f32 = jnp.float32
bf16 = jnp.bfloat16


def exchange(blocks, axis):
    return lax.all_to_all(blocks, axis, 0, 0)


def spread(block, axis, count):
    return exchange(jnp.broadcast_to(block[None], (count,) + block.shape), axis)


def partner(block):
    return lax.ppermute(block, "c", SWAP)


def shift(block, axis, by):
    return lax.ppermute(block, axis, [(i, (i + by) % 4) for i in range(4)])


def hidden_kernel(seat, mine, left, right, far, own_cols, other_cols, out, held):
    x, y, c = seat[0], seat[1], seat[2]
    rows, feats = mine.shape
    cols = own_cols.shape[0] // NY
    for k, block in enumerate((mine, left, right, far)):
        held[k, :rows] = block[...]
        held[k, rows:] = jnp.zeros((64 - rows, feats), bf16)
    blocks = held[...].reshape(NX * 64, feats)

    def times(weights):
        return lax.dot_general(weights, blocks, (((1,), (1,)), ((), ())), preferred_element_type=f32)

    own, other = times(own_cols[...]), times(other_cols[...])
    first, second = jnp.where(c == 0, own, other), jnp.where(c == 0, other, own)
    beside = y + 1 - 2 * lax.rem(y, 2)
    for k, off in enumerate((0, 3, 1, 2)):
        both = jnp.concatenate([first[:, 64 * k : 64 * k + 64], second[:, 64 * k : 64 * k + 64]], axis=1)
        for j, at in enumerate((y, beside, 3 - y, 3 - beside)):
            out[lax.rem(x + off, NX), at] = both[j * cols : (j + 1) * cols]


def partial_hidden(seat, blocks, own_cols, other_cols, cols):
    vmem = pl.BlockSpec(memory_space=pltpu.VMEM)
    return pl.pallas_call(
        hidden_kernel,
        out_shape=jax.ShapeDtypeStruct((NX, NY, cols, 128), f32),
        in_specs=[pl.BlockSpec(memory_space=pltpu.SMEM)] + [vmem] * 6,
        out_specs=vmem,
        scratch_shapes=[pltpu.VMEM((NX, 64, blocks[0].shape[1]), bf16)],
        cost_estimate=pl.CostEstimate(flops=330_000_000, bytes_accessed=3_400_000, transcendentals=0),
    )(seat, *blocks, own_cols, other_cols)


def centre_kernel(centres, own, received, out):
    wide = centres[...].astype(f32)
    cinv = lax.rsqrt(jnp.sum(wide * wide, axis=1, keepdims=True) + norm_eps)
    unit_centre = wide * cinv
    gunit = own[...] + received[...]
    out[...] = cinv * (gunit - unit_centre * jnp.sum(unit_centre * gunit, axis=1, keepdims=True))


def centre_gradient(centres, own, received):
    rows, emb = centres.shape
    block = pl.BlockSpec(memory_space=pltpu.VMEM)
    return pl.pallas_call(
        centre_kernel,
        out_shape=jax.ShapeDtypeStruct((rows, emb), f32),
        in_specs=[block] * 3,
        out_specs=block,
        cost_estimate=pl.CostEstimate(flops=3_000_000, bytes_accessed=3_700_000, transcendentals=512),
    )(centres, own, received)


def split_pair(value):
    high = lax.reduce_precision(value, 8, 7)
    return high.astype(bf16), (value - high).astype(bf16)


def step_of(features, proj_in, proj_out, centres, labels):
    rows, _ = features.shape
    cols = proj_in.shape[1]
    emb = proj_out.shape[1]
    cen = centres.shape[0]
    images = NX * NY * rows
    zi, xi, yi, ci = (lax.axis_index(a) for a in ("z", "x", "y", "c"))

    from_left = shift(features, "x", 1)
    from_right = shift(features, "x", 3)
    own_cols = proj_in.T
    own_out = spread(lax.dynamic_slice_in_dim(proj_out, ci * (emb // 2), emb // 2, 1), "z", NZ)
    own_cols = jnp.concatenate([own_cols, lax.ppermute(own_cols, "y", [(0, 1), (1, 0), (2, 3), (3, 2)])], axis=0)
    own_cols = jnp.concatenate([own_cols, lax.ppermute(own_cols, "y", [(0, 3), (3, 0), (1, 2), (2, 1)])], axis=0)
    from_far = shift(from_left, "x", 1)
    other_cols = partner(own_cols)
    seat = jnp.stack([xi, yi, ci]).astype(jnp.int32)
    part = partial_hidden(seat, (features, from_left, from_right, from_far), own_cols, other_cols, cols)
    part = exchange(part, "x").reshape(NZ, cols, 128)

    part, labels = lax.optimization_barrier((part, labels))
    all_labels = lax.dynamic_update_slice_in_dim(jnp.zeros(NY * rows, jnp.int32), labels, yi * rows, 0)
    all_labels = lax.psum(all_labels, "y")
    all_labels = lax.dynamic_update_slice_in_dim(jnp.zeros(images, jnp.int32), all_labels, xi * NY * rows, 0)
    all_labels = lax.psum(all_labels, "x")
    all_labels = all_labels.reshape(images, 1)
    wide = centres.astype(f32)
    cinv = lax.rsqrt(jnp.sum(wide * wide, axis=1) + norm_eps)
    unit_centre = wide * cinv[:, None]
    own_low = unit_centre.astype(bf16)
    low = jnp.concatenate([own_low, partner(own_low)], axis=0)
    chip = ((zi * NX + xi) * NY + yi) * NC
    step = jnp.arange(cen, dtype=jnp.int32)
    position = jnp.concatenate([(chip + ci) * cen + step, (chip + 1 - ci) * cen + step])
    target = all_labels == position[None, :]

    other_out = partner(own_out)
    hidden = jnp.sum(exchange(part, "z"), axis=0).astype(bf16)
    hidden = spread(hidden, "z", NZ).reshape(NZ * cols, 128)

    def over_rows(left, right):
        return lax.dot_general(left, right, (((0,), (0,)), ((), ())), preferred_element_type=f32)

    def embed_with(out_rows):
        left = over_rows(hidden[:, :rows], out_rows[:, :cols].reshape(NZ * cols, emb // 2))
        return left + over_rows(hidden[:, 64 : 64 + rows], out_rows[:, cols:].reshape(NZ * cols, emb // 2))

    own, other = embed_with(own_out), embed_with(other_out)
    embed = jnp.concatenate([jnp.where(ci == 0, own, other), jnp.where(ci == 0, other, own)], axis=1)
    inverse = lax.rsqrt(jnp.sum(embed * embed, axis=1) + norm_eps)
    unit = embed * inverse[:, None]
    units = spread(unit.astype(bf16), XY, NX * NY).reshape(images, emb)

    chosen = jnp.dot(target.astype(bf16), low, preferred_element_type=f32).astype(bf16)
    chosen, units = lax.optimization_barrier((chosen, units))
    chosen = exchange(chosen.reshape(NX * NY, rows, emb), XY)
    chosen = jnp.sum(chosen.astype(f32), axis=0)

    cos_m = jnp.cos(f32(margin_angle))
    sin_m = jnp.sin(f32(margin_angle))
    cosine = lax.dot_general(units, low, (((1,), (1,)), ((), ())), preferred_element_type=f32)
    inner = 1.0 - cosine * cosine
    sine = jnp.sqrt(jnp.maximum(inner, sine_floor))
    logit = jnp.where(target, scale_logit * (cosine * cos_m - sine * sin_m), scale_logit * cosine)
    exps = jnp.exp(logit)
    slope = cos_m + jnp.where(inner > sine_floor, sin_m * cosine / sine, 0.0)
    rest = jnp.where(target, 0.0, exps)
    rest_sum = jnp.sum(rest, axis=1)
    rest_cos = jnp.sum(rest * cosine, axis=1)
    hit = jnp.sum(jnp.where(target, exps, 0.0), axis=1)
    hit_slope = jnp.sum(jnp.where(target, slope, 0.0), axis=1)
    hit_turn = jnp.sum(jnp.where(target, slope * cosine, 0.0), axis=1)

    pull = jnp.dot(lax.optimization_barrier(rest.astype(bf16)), low, preferred_element_type=f32).astype(bf16).reshape(NX * NY, rows, emb)
    tall = images // 128
    totals = jnp.concatenate(split_pair((rest_sum + hit).reshape(tall, 128)), axis=0)
    totals = jnp.pad(totals, ((0, 16 - 2 * tall), (0, 0))).reshape(4, emb)
    totals = jnp.broadcast_to(totals[None], (NX * NY, 4, emb))
    owned = jnp.stack([rest_sum, hit, rest_cos, hit_slope, hit_turn]).reshape(5, NX * NY, rows)
    owned = jnp.pad(owned.transpose(1, 0, 2), ((0, 0), (0, 0), (0, 64 - rows)))
    owned = jnp.concatenate(split_pair(owned), axis=1).reshape(NX * NY, 640)
    owned = jnp.pad(owned, ((0, 0), (0, 4 * emb - 640))).reshape(NX * NY, 4, emb)
    pull = jnp.concatenate([pull, totals, owned], axis=1)
    pull = exchange(pull, XY)
    pull = jnp.sum(pull.astype(f32), axis=0)
    totals = pull[rows : rows + 4].reshape(16, 128)
    totals = totals[:tall] + totals[tall : 2 * tall]
    owned = pull[rows + 4 :].reshape(4 * emb)[:640].reshape(10, 64)
    owned = jnp.pad(owned[:5] + owned[5:], ((0, 0), (0, 64)))

    width = emb // NZ

    def by_column(block):
        block = block.astype(bf16).reshape(4, rows // 4, NZ, width)
        return block.transpose(2, 1, 0, 3).reshape(NZ, rows // 4, 4 * width)

    pull = pull[:rows]
    common = jnp.concatenate(split_pair(totals) + split_pair(owned), axis=0)
    common = jnp.broadcast_to(common[None], (NZ,) + common.shape)
    pack = jnp.concatenate([by_column(pull), by_column(chosen), common], axis=1)
    pack = exchange(pack, "z")
    pack = jnp.sum(pack.astype(f32), axis=0)

    def by_row(block):
        return block.reshape(rows // 4, 4, width).transpose(1, 0, 2).reshape(rows, width)

    quarter = rows // 4
    pull, chosen = by_row(pack[:quarter]), by_row(pack[quarter : 2 * quarter])
    common = pack[2 * quarter :]
    total = (common[:tall] + common[tall : 2 * tall]).reshape(images, 1)
    owned = common[2 * tall : 2 * tall + 5, :rows] + common[2 * tall + 5 :, :rows]
    own_rest, own_hit, own_cos, own_slope, own_turn = (owned[k] for k in range(5))

    cosine_t = lax.dot_general(low, units, (((1,), (1,)), ((), ())), preferred_element_type=f32)
    target_t = position[:, None] == all_labels.reshape(1, images)
    rest_t = jnp.where(target_t, 0.0, jnp.exp(scale_logit * cosine_t)).astype(bf16)
    joined = lax.optimization_barrier(jnp.concatenate([rest_t, target_t.astype(bf16)], axis=1))
    weight = scale_logit * hit_slope[:, None] * (hit[:, None] / total - 1.0)
    scaled = (units.astype(f32) * (scale_logit / total)).astype(bf16)
    aimed = (units.astype(f32) * weight).astype(bf16)
    scaled = lax.optimization_barrier(jnp.concatenate([scaled, aimed], axis=0))

    def gradient_of(part):
        return jnp.dot(joined[part], scaled, preferred_element_type=f32)

    received = partner(gradient_of(slice(cen, None)))
    centre_grad = centre_gradient(centres, gradient_of(slice(0, cen)), received)

    own_scale = scale_logit / (own_rest + own_hit)
    dunit = own_scale[:, None] * (pull - (own_rest * own_slope)[:, None] * chosen)
    along = own_scale * (own_cos - own_rest * own_turn)
    unit_cols = lax.dynamic_slice_in_dim(unit, zi * width, width, 1)
    emb_grad = inverse[:, None] * (dunit - unit_cols * along[:, None])
    return (centre_grad, emb_grad)


def solution(mesh):
    fine = Mesh(np.asarray(mesh.devices).reshape(NZ, NX, NY, NC), ("z", "x", "y", "c"))
    img = ("x", "y", "c")
    every = ("z", "x", "y", "c")
    return jax.shard_map(
        step_of,
        mesh=fine,
        in_specs=(P(img, "z"), P("z", img), P("z", None), P(every, None), P(img)),
        out_specs=(P(every, None), P(img, "z")),
        check_vma=False,
    )
```

```python
import jax
import jax.numpy as jnp
import numpy as np
from jax import lax
from jax.experimental import pallas as pl
from jax.experimental.pallas import tpu as pltpu
from jax.sharding import Mesh, PartitionSpec as P


norm_eps = 1e-06
scale_logit = 64.0
margin_angle = 0.5
sine_floor = 0.04

NZ, NX, NY, NC = 16, 4, 4, 2
XY = ("x", "y")
SWAP = [(0, 1), (1, 0)]
f32 = jnp.float32
bf16 = jnp.bfloat16


def exchange(blocks, axis):
    return lax.all_to_all(blocks, axis, 0, 0)


def spread(block, axis, count):
    return exchange(jnp.broadcast_to(block[None], (count,) + block.shape), axis)


def partner(block):
    return lax.ppermute(block, "c", SWAP)


def shift(block, axis, by):
    return lax.ppermute(block, axis, [(i, (i + by) % 4) for i in range(4)])


def hidden_kernel(seat, mine, left, right, far, own_cols, other_cols, out, held):
    x, y, c = seat[0], seat[1], seat[2]
    rows, feats = mine.shape
    cols = own_cols.shape[0] // NY
    for k, block in enumerate((mine, left, right, far)):
        held[k, :rows] = block[...]
        held[k, rows:] = jnp.zeros((64 - rows, feats), bf16)
    blocks = held[...].reshape(NX * 64, feats)

    def times(weights):
        return lax.dot_general(weights, blocks, (((1,), (1,)), ((), ())), preferred_element_type=f32)

    own, other = times(own_cols[...]), times(other_cols[...])
    first, second = jnp.where(c == 0, own, other), jnp.where(c == 0, other, own)
    beside = y + 1 - 2 * lax.rem(y, 2)
    for k, off in enumerate((0, 3, 1, 2)):
        both = jnp.concatenate([first[:, 64 * k : 64 * k + 64], second[:, 64 * k : 64 * k + 64]], axis=1)
        for j, at in enumerate((y, beside, 3 - y, 3 - beside)):
            out[lax.rem(x + off, NX), at] = both[j * cols : (j + 1) * cols]


def partial_hidden(seat, blocks, own_cols, other_cols, cols):
    vmem = pl.BlockSpec(memory_space=pltpu.VMEM)
    return pl.pallas_call(
        hidden_kernel,
        out_shape=jax.ShapeDtypeStruct((NX, NY, cols, 128), f32),
        in_specs=[pl.BlockSpec(memory_space=pltpu.SMEM)] + [vmem] * 6,
        out_specs=vmem,
        scratch_shapes=[pltpu.VMEM((NX, 64, blocks[0].shape[1]), bf16)],
        cost_estimate=pl.CostEstimate(flops=330_000_000, bytes_accessed=3_400_000, transcendentals=0),
    )(seat, *blocks, own_cols, other_cols)


def partner_kernel(joined, scaled, out):
    out[...] = jnp.dot(joined[...], scaled[...], preferred_element_type=f32)


def centre_kernel(joined, scaled, centres, received, out, held, arrived):
    size = out.shape[0]
    copy = pltpu.make_async_copy(received, held, arrived)
    pl.when(pl.program_id(0) == 0)(copy.start)
    wide = centres[...].astype(f32)
    cinv = lax.rsqrt(jnp.sum(wide * wide, axis=1, keepdims=True) + norm_eps)
    unit_centre = wide * cinv
    gunit = jnp.dot(joined[...], scaled[...], preferred_element_type=f32)
    pl.when(pl.program_id(0) == 0)(copy.wait)
    gunit = gunit + held[pl.ds(pl.multiple_of(pl.program_id(0) * size, size), size), :]
    out[...] = cinv * (gunit - unit_centre * jnp.sum(unit_centre * gunit, axis=1, keepdims=True))


STEPS = 4


def over_centres(kernel, first, joined, scaled, *rest):
    rows, emb = joined.shape[0] // NC, scaled.shape[1]
    whole = pl.BlockSpec(memory_space=pltpu.VMEM)
    block = pl.BlockSpec((rows // STEPS, emb), lambda i: (i, 0))
    return pl.pallas_call(
        kernel,
        out_shape=jax.ShapeDtypeStruct((rows, emb), f32),
        grid=(STEPS,),
        in_specs=[pl.BlockSpec((rows // STEPS, joined.shape[1]), lambda i: (i + first, 0)), whole] + [block, pl.BlockSpec(memory_space=pl.ANY)][: len(rest)],
        out_specs=block,
        scratch_shapes=[pltpu.VMEM((rows, emb), f32), pltpu.SemaphoreType.DMA][: len(rest)],
        cost_estimate=pl.CostEstimate(flops=940_000_000, bytes_accessed=4_500_000, transcendentals=512),
    )(joined, scaled, *rest)


def split_pair(value):
    high = lax.reduce_precision(value, 8, 7)
    return high.astype(bf16), (value - high).astype(bf16)


def step_of(features, proj_in, proj_out, centres, labels):
    rows, _ = features.shape
    cols = proj_in.shape[1]
    emb = proj_out.shape[1]
    cen = centres.shape[0]
    images = NX * NY * rows
    zi, xi, yi, ci = (lax.axis_index(a) for a in ("z", "x", "y", "c"))

    from_left = shift(features, "x", 1)
    from_right = shift(features, "x", 3)
    own_cols = proj_in.T
    own_out = spread(lax.dynamic_slice_in_dim(proj_out, ci * (emb // 2), emb // 2, 1), "z", NZ)
    own_cols = jnp.concatenate([own_cols, lax.ppermute(own_cols, "y", [(0, 1), (1, 0), (2, 3), (3, 2)])], axis=0)
    own_cols = jnp.concatenate([own_cols, lax.ppermute(own_cols, "y", [(0, 3), (3, 0), (1, 2), (2, 1)])], axis=0)
    from_far = shift(from_left, "x", 1)
    other_cols = partner(own_cols)
    seat = jnp.stack([xi, yi, ci]).astype(jnp.int32)
    part = partial_hidden(seat, (features, from_left, from_right, from_far), own_cols, other_cols, cols)
    part, labels = lax.optimization_barrier((part, labels))
    all_labels = lax.dynamic_update_slice_in_dim(jnp.zeros(NY * rows, jnp.int32), labels, yi * rows, 0)
    all_labels = lax.psum(all_labels, "y")
    all_labels = lax.dynamic_update_slice_in_dim(jnp.zeros(images, jnp.int32), all_labels, xi * NY * rows, 0)
    all_labels = lax.psum(all_labels, "x")
    part = exchange(part, "x").reshape(NZ, cols, 128)

    all_labels = all_labels.reshape(images, 1)
    wide = centres.astype(f32)
    cinv = lax.rsqrt(jnp.sum(wide * wide, axis=1) + norm_eps)
    unit_centre = wide * cinv[:, None]
    own_low = unit_centre.astype(bf16)
    low = partner(own_low)
    low = jnp.concatenate([own_low, low], axis=0)
    chip = ((zi * NX + xi) * NY + yi) * NC
    step = jnp.arange(cen, dtype=jnp.int32)
    position = jnp.concatenate([(chip + ci) * cen + step, (chip + 1 - ci) * cen + step])
    target = all_labels == position[None, :]

    other_out = partner(own_out)
    hidden = jnp.sum(exchange(part, "z"), axis=0).astype(bf16)
    hidden = spread(hidden, "z", NZ).reshape(NZ * cols, 128)

    def over_rows(left, right):
        return lax.dot_general(left, right, (((0,), (0,)), ((), ())), preferred_element_type=f32)

    def embed_with(out_rows):
        left = over_rows(hidden[:, :rows], out_rows[:, :cols].reshape(NZ * cols, emb // 2))
        return left + over_rows(hidden[:, 64 : 64 + rows], out_rows[:, cols:].reshape(NZ * cols, emb // 2))

    own, other = embed_with(own_out), embed_with(other_out)
    embed = jnp.concatenate([jnp.where(ci == 0, own, other), jnp.where(ci == 0, other, own)], axis=1)
    inverse = lax.rsqrt(jnp.sum(embed * embed, axis=1) + norm_eps)
    unit = embed * inverse[:, None]
    units = spread(unit.astype(bf16), XY, NX * NY).reshape(images, emb)

    chosen = jnp.dot(target.astype(bf16), low, preferred_element_type=f32).astype(bf16)
    chosen, units = lax.optimization_barrier((chosen, units))
    chosen = exchange(chosen.reshape(NX * NY, rows, emb), XY)
    chosen = jnp.sum(chosen.astype(f32), axis=0)

    cos_m = jnp.cos(f32(margin_angle))
    sin_m = jnp.sin(f32(margin_angle))
    cosine = lax.dot_general(units, low, (((1,), (1,)), ((), ())), preferred_element_type=f32)
    inner = 1.0 - cosine * cosine
    sine = jnp.sqrt(jnp.maximum(inner, sine_floor))
    logit = jnp.where(target, scale_logit * (cosine * cos_m - sine * sin_m), scale_logit * cosine)
    exps = jnp.exp(logit)
    slope = cos_m + jnp.where(inner > sine_floor, sin_m * cosine / sine, 0.0)
    rest = jnp.where(target, 0.0, exps)
    rest_sum = jnp.sum(rest, axis=1)
    rest_cos = jnp.sum(rest * cosine, axis=1)
    hit = jnp.sum(jnp.where(target, exps, 0.0), axis=1)
    hit_slope = jnp.sum(jnp.where(target, slope, 0.0), axis=1)
    hit_turn = jnp.sum(jnp.where(target, slope * cosine, 0.0), axis=1)

    pull = jnp.dot(lax.optimization_barrier(rest.astype(bf16)), low, preferred_element_type=f32).astype(bf16).reshape(NX * NY, rows, emb)
    tall = images // 128
    totals = jnp.concatenate(split_pair((rest_sum + hit).reshape(tall, 128)), axis=0)
    totals = jnp.pad(totals, ((0, 16 - 2 * tall), (0, 0))).reshape(4, emb)
    totals = jnp.broadcast_to(totals[None], (NX * NY, 4, emb))
    owned = jnp.stack([rest_sum, hit, rest_cos, hit_slope, hit_turn]).reshape(5, NX * NY, rows)
    owned = jnp.pad(owned.transpose(1, 0, 2), ((0, 0), (0, 0), (0, 64 - rows)))
    owned = jnp.concatenate(split_pair(owned), axis=1).reshape(NX * NY, 640)
    owned = jnp.pad(owned, ((0, 0), (0, 4 * emb - 640))).reshape(NX * NY, 4, emb)
    pull = jnp.concatenate([pull, totals, owned], axis=1)
    pull = exchange(pull, XY)
    pull = jnp.sum(pull.astype(f32), axis=0)
    totals = pull[rows : rows + 4].reshape(16, 128)
    totals = totals[:tall] + totals[tall : 2 * tall]
    owned = pull[rows + 4 :].reshape(4 * emb)[:640].reshape(10, 64)
    owned = owned[:5] + owned[5:]

    width = emb // NZ

    def by_column(block):
        block = block.astype(bf16).reshape(4, rows // 4, NZ, width)
        return block.transpose(2, 1, 0, 3).reshape(NZ, rows // 4, 4 * width)

    pull = pull[:rows]
    common = jnp.concatenate(split_pair(totals) + (jnp.concatenate(split_pair(owned), axis=1),), axis=0)
    common = jnp.broadcast_to(common[None], (NZ,) + common.shape)
    pack = jnp.concatenate([by_column(pull), by_column(chosen), common], axis=1)
    pack = exchange(pack, "z")
    pack = jnp.sum(pack.astype(f32), axis=0)

    def by_row(block):
        return block.reshape(rows // 4, 4, width).transpose(1, 0, 2).reshape(rows, width)

    quarter = rows // 4
    pull, chosen = by_row(pack[:quarter]), by_row(pack[quarter : 2 * quarter])
    common = pack[2 * quarter :]
    total = (common[:tall] + common[tall : 2 * tall]).reshape(images, 1)
    owned = common[2 * tall :, :rows] + common[2 * tall :, 64 : 64 + rows]
    own_rest, own_hit, own_cos, own_slope, own_turn = (owned[k] for k in range(5))

    cosine_t = lax.dot_general(low, units, (((1,), (1,)), ((), ())), preferred_element_type=f32)
    target_t = position[:, None] == all_labels.reshape(1, images)
    rest_t = jnp.where(target_t, 0.0, jnp.exp(scale_logit * cosine_t)).astype(bf16)
    joined = lax.optimization_barrier(jnp.concatenate([rest_t, target_t.astype(bf16)], axis=1))
    weight = scale_logit * hit_slope[:, None] * (hit[:, None] / total - 1.0)
    scaled = (units.astype(f32) * (scale_logit / total)).astype(bf16)
    aimed = (units.astype(f32) * weight).astype(bf16)
    scaled = lax.optimization_barrier(jnp.concatenate([scaled, aimed], axis=0))

    received = partner(over_centres(partner_kernel, STEPS, joined, scaled))
    centre_grad = over_centres(centre_kernel, 0, joined, scaled, centres, received)

    own_scale = scale_logit / (own_rest + own_hit)
    dunit = own_scale[:, None] * (pull - (own_rest * own_slope)[:, None] * chosen)
    along = own_scale * (own_cos - own_rest * own_turn)
    unit_cols = lax.dynamic_slice_in_dim(unit, zi * width, width, 1)
    emb_grad = inverse[:, None] * (dunit - unit_cols * along[:, None])
    return (centre_grad, emb_grad)


def solution(mesh):
    fine = Mesh(np.asarray(mesh.devices).reshape(NZ, NX, NY, NC), ("z", "x", "y", "c"))
    img = ("x", "y", "c")
    every = ("z", "x", "y", "c")
    return jax.shard_map(
        step_of,
        mesh=fine,
        in_specs=(P(img, "z"), P("z", img), P("z", None), P(every, None), P(img)),
        out_specs=(P(every, None), P(img, "z")),
        check_vma=False,
    )
```

```python
import jax
import jax.numpy as jnp
import numpy as np
from jax import lax
from jax.experimental import pallas as pl
from jax.experimental.pallas import tpu as pltpu
from jax.sharding import Mesh, PartitionSpec as P


norm_eps = 1e-06
scale_logit = 64.0
margin_angle = 0.5
sine_floor = 0.04

NZ, NX, NY, NC = 16, 4, 4, 2
XY = ("x", "y")
SWAP = [(0, 1), (1, 0)]
f32 = jnp.float32
bf16 = jnp.bfloat16


def exchange(blocks, axis):
    return lax.all_to_all(blocks, axis, 0, 0)


def spread(block, axis, count):
    return exchange(jnp.broadcast_to(block[None], (count,) + block.shape), axis)


def partner(block):
    return lax.ppermute(block, "c", SWAP)


def shift(block, axis, by):
    return lax.ppermute(block, axis, [(i, (i + by) % 4) for i in range(4)])


def hidden_kernel(seat, mine, left, right, far, own_cols, other_cols, out, held):
    x, y, c = seat[0], seat[1], seat[2]
    rows, feats = mine.shape
    cols = own_cols.shape[0] // NY
    for k, block in enumerate((mine, left, right, far)):
        held[k, :rows] = block[...]
        held[k, rows:] = jnp.zeros((64 - rows, feats), bf16)
    blocks = held[...].reshape(NX * 64, feats)

    def times(weights):
        return lax.dot_general(weights, blocks, (((1,), (1,)), ((), ())), preferred_element_type=f32)

    own, other = times(own_cols[...]), times(other_cols[...])
    first, second = jnp.where(c == 0, own, other), jnp.where(c == 0, other, own)
    beside = y + 1 - 2 * lax.rem(y, 2)
    for k, off in enumerate((0, 3, 1, 2)):
        both = jnp.concatenate([first[:, 64 * k : 64 * k + 64], second[:, 64 * k : 64 * k + 64]], axis=1)
        for j, at in enumerate((y, beside, 3 - y, 3 - beside)):
            out[lax.rem(x + off, NX), at] = both[j * cols : (j + 1) * cols]


def partial_hidden(seat, blocks, own_cols, other_cols, cols):
    vmem = pl.BlockSpec(memory_space=pltpu.VMEM)
    return pl.pallas_call(
        hidden_kernel,
        out_shape=jax.ShapeDtypeStruct((NX, NY, cols, 128), f32),
        in_specs=[pl.BlockSpec(memory_space=pltpu.SMEM)] + [vmem] * 6,
        out_specs=vmem,
        scratch_shapes=[pltpu.VMEM((NX, 64, blocks[0].shape[1]), bf16)],
        cost_estimate=pl.CostEstimate(flops=330_000_000, bytes_accessed=3_400_000, transcendentals=0),
    )(seat, *blocks, own_cols, other_cols)


def centre_kernel(centres, own, received, out):
    wide = centres[...].astype(f32)
    cinv = lax.rsqrt(jnp.sum(wide * wide, axis=1, keepdims=True) + norm_eps)
    unit_centre = wide * cinv
    gunit = own[...] + received[...]
    out[...] = cinv * (gunit - unit_centre * jnp.sum(unit_centre * gunit, axis=1, keepdims=True))


def centre_gradient(centres, own, received):
    rows, emb = centres.shape
    block = pl.BlockSpec(memory_space=pltpu.VMEM)
    return pl.pallas_call(
        centre_kernel,
        out_shape=jax.ShapeDtypeStruct((rows, emb), f32),
        in_specs=[block] * 3,
        out_specs=block,
        cost_estimate=pl.CostEstimate(flops=3_000_000, bytes_accessed=3_700_000, transcendentals=512),
    )(centres, own, received)


def split_pair(value):
    high = lax.reduce_precision(value, 8, 7)
    return high.astype(bf16), (value - high).astype(bf16)


def step_of(features, proj_in, proj_out, centres, labels):
    rows, _ = features.shape
    cols = proj_in.shape[1]
    emb = proj_out.shape[1]
    cen = centres.shape[0]
    images = NX * NY * rows
    zi, xi, yi, ci = (lax.axis_index(a) for a in ("z", "x", "y", "c"))

    from_left = shift(features, "x", 1)
    from_right = shift(features, "x", 3)
    own_cols = proj_in.T
    own_out = spread(lax.dynamic_slice_in_dim(proj_out, ci * (emb // 2), emb // 2, 1), "z", NZ)
    own_cols = jnp.concatenate([own_cols, lax.ppermute(own_cols, "y", [(0, 1), (1, 0), (2, 3), (3, 2)])], axis=0)
    own_cols = jnp.concatenate([own_cols, lax.ppermute(own_cols, "y", [(0, 3), (3, 0), (1, 2), (2, 1)])], axis=0)
    from_far = shift(from_left, "x", 1)
    other_cols = partner(own_cols)
    seat = jnp.stack([xi, yi, ci]).astype(jnp.int32)
    part = partial_hidden(seat, (features, from_left, from_right, from_far), own_cols, other_cols, cols)
    part = exchange(part, "x").reshape(NZ, cols, 128)

    part, labels = lax.optimization_barrier((part, labels))
    all_labels = lax.dynamic_update_slice_in_dim(jnp.zeros(NY * rows, jnp.int32), labels, yi * rows, 0)
    all_labels = lax.psum(all_labels, "y")
    all_labels = lax.dynamic_update_slice_in_dim(jnp.zeros(images, jnp.int32), all_labels, xi * NY * rows, 0)
    all_labels = lax.psum(all_labels, "x")
    all_labels = all_labels.reshape(images, 1)
    wide = centres.astype(f32)
    cinv = lax.rsqrt(jnp.sum(wide * wide, axis=1) + norm_eps)
    unit_centre = wide * cinv[:, None]
    own_low = unit_centre.astype(bf16)
    low = jnp.concatenate([own_low, partner(own_low)], axis=0)
    chip = ((zi * NX + xi) * NY + yi) * NC
    step = jnp.arange(cen, dtype=jnp.int32)
    position = jnp.concatenate([(chip + ci) * cen + step, (chip + 1 - ci) * cen + step])
    target = all_labels == position[None, :]

    other_out = partner(own_out)
    hidden = jnp.sum(exchange(part, "z"), axis=0).astype(bf16)
    hidden = spread(hidden, "z", NZ).reshape(NZ * cols, 128)

    def over_rows(left, right):
        return lax.dot_general(left, right, (((0,), (0,)), ((), ())), preferred_element_type=f32)

    def embed_with(out_rows):
        left = over_rows(hidden[:, :rows], out_rows[:, :cols].reshape(NZ * cols, emb // 2))
        return left + over_rows(hidden[:, 64 : 64 + rows], out_rows[:, cols:].reshape(NZ * cols, emb // 2))

    own, other = embed_with(own_out), embed_with(other_out)
    embed = jnp.concatenate([jnp.where(ci == 0, own, other), jnp.where(ci == 0, other, own)], axis=1)
    inverse = lax.rsqrt(jnp.sum(embed * embed, axis=1) + norm_eps)
    unit = embed * inverse[:, None]
    units = spread(unit.astype(bf16), XY, NX * NY).reshape(images, emb)

    chosen = jnp.dot(target.astype(bf16), low, preferred_element_type=f32).astype(bf16)
    chosen, units = lax.optimization_barrier((chosen, units))
    chosen = exchange(chosen.reshape(NX * NY, rows, emb), XY)
    chosen = jnp.sum(chosen.astype(f32), axis=0)

    cos_m = jnp.cos(f32(margin_angle))
    sin_m = jnp.sin(f32(margin_angle))
    cosine = lax.dot_general(units, low, (((1,), (1,)), ((), ())), preferred_element_type=f32)
    inner = 1.0 - cosine * cosine
    sine = jnp.sqrt(jnp.maximum(inner, sine_floor))
    logit = jnp.where(target, scale_logit * (cosine * cos_m - sine * sin_m), scale_logit * cosine)
    exps = jnp.exp(logit)
    slope = cos_m + jnp.where(inner > sine_floor, sin_m * cosine / sine, 0.0)
    rest = jnp.where(target, 0.0, exps)
    rest_sum = jnp.sum(rest, axis=1)
    rest_cos = jnp.sum(rest * cosine, axis=1)
    hit = jnp.sum(jnp.where(target, exps, 0.0), axis=1)
    hit_slope = jnp.sum(jnp.where(target, slope, 0.0), axis=1)
    hit_turn = jnp.sum(jnp.where(target, slope * cosine, 0.0), axis=1)

    pull = jnp.dot(lax.optimization_barrier(rest.astype(bf16)), low, preferred_element_type=f32).astype(bf16).reshape(NX * NY, rows, emb)
    tall = images // 128
    shared = jnp.concatenate([rest_sum, hit + rest_sum]).reshape(2 * tall, 128)
    shared = jnp.concatenate(split_pair(shared), axis=0)
    owned = jnp.stack([rest_cos, hit_slope, hit_turn]).reshape(3, NX * NY, rows)
    owned = jnp.pad(owned.transpose(1, 0, 2), ((0, 0), (0, 0), (0, 64 - rows)))
    owned = jnp.pad(jnp.concatenate(split_pair(owned), axis=2), ((0, 0), (0, 1), (0, 0)))
    shared = jnp.broadcast_to(shared[None], (NX * NY,) + shared.shape)
    extra = jnp.concatenate([shared, owned], axis=1).reshape(NX * NY, 8, emb)
    pull = jnp.concatenate([pull, extra], axis=1)
    pull = exchange(pull, XY)
    pull = jnp.sum(pull.astype(f32), axis=0)
    extra = pull[rows:].reshape(32, 128)
    shared = extra[: 2 * tall] + extra[2 * tall : 4 * tall]
    owned = extra[4 * tall : 4 * tall + 3, :64] + extra[4 * tall : 4 * tall + 3, 64:]

    width = emb // NZ

    def by_column(block):
        block = block.astype(bf16).reshape(4, rows // 4, NZ, width)
        return block.transpose(2, 1, 0, 3).reshape(NZ, rows // 4, 4 * width)

    pull = pull[:rows]
    common = jnp.concatenate(split_pair(shared) + (jnp.concatenate(split_pair(owned), axis=1),), axis=0)
    common = jnp.broadcast_to(common[None], (NZ,) + common.shape)
    pack = jnp.concatenate([by_column(pull), by_column(chosen), common], axis=1)
    pack = exchange(pack, "z")
    pack = jnp.sum(pack.astype(f32), axis=0)

    def by_row(block):
        return block.reshape(rows // 4, 4, width).transpose(1, 0, 2).reshape(rows, width)

    quarter = rows // 4
    pull, chosen = by_row(pack[:quarter]), by_row(pack[quarter : 2 * quarter])
    common = pack[2 * quarter :]
    shared = (common[: 2 * tall] + common[2 * tall : 4 * tall]).reshape(2, images)
    own_rest, own_total = lax.dynamic_slice_in_dim(shared, (xi * NY + yi) * rows, rows, 1)
    owned = common[4 * tall :, :rows] + common[4 * tall :, 64 : 64 + rows]
    own_cos, own_slope, own_turn = (owned[k] for k in range(3))

    cosine_t = lax.dot_general(low, units, (((1,), (1,)), ((), ())), preferred_element_type=f32)
    target_t = position[:, None] == all_labels.reshape(1, images)
    rest_t = jnp.where(target_t, 0.0, jnp.exp(scale_logit * cosine_t)).astype(bf16)
    rest_t = lax.optimization_barrier(rest_t)
    scaled = (units.astype(f32) * (scale_logit / shared[1])[:, None]).astype(bf16)
    at_target = -hit_slope * shared[0]

    def gradient_of(part):
        mixed = jnp.where(target_t[part], at_target[None, :], rest_t[part].astype(f32)).astype(bf16)
        return jnp.dot(mixed, scaled, preferred_element_type=f32)

    received = partner(gradient_of(slice(cen, None)))
    centre_grad = centre_gradient(centres, gradient_of(slice(0, cen)), received)

    own_scale = scale_logit / own_total
    dunit = own_scale[:, None] * (pull - (own_rest * own_slope)[:, None] * chosen)
    along = own_scale * (own_cos - own_rest * own_turn)
    unit_cols = lax.dynamic_slice_in_dim(unit, zi * width, width, 1)
    emb_grad = inverse[:, None] * (dunit - unit_cols * along[:, None])
    return (centre_grad, emb_grad)


def solution(mesh):
    fine = Mesh(np.asarray(mesh.devices).reshape(NZ, NX, NY, NC), ("z", "x", "y", "c"))
    img = ("x", "y", "c")
    every = ("z", "x", "y", "c")
    return jax.shard_map(
        step_of,
        mesh=fine,
        in_specs=(P(img, "z"), P("z", img), P("z", None), P(every, None), P(img)),
        out_specs=(P(every, None), P(img, "z")),
        check_vma=False,
    )
```

```python
import jax
import jax.numpy as jnp
import numpy as np
from jax import lax
from jax.experimental import pallas as pl
from jax.experimental.pallas import tpu as pltpu
from jax.sharding import Mesh, PartitionSpec as P


norm_eps = 1e-06
scale_logit = 64.0
margin_angle = 0.5
sine_floor = 0.04

NZ, NX, NY, NC = 16, 4, 4, 2
XY = ("x", "y")
SWAP = [(0, 1), (1, 0)]
NEAR = [(0, 1), (1, 0), (2, 3), (3, 2)]
f32 = jnp.float32
bf16 = jnp.bfloat16


def exchange(blocks, axis):
    return lax.all_to_all(blocks, axis, 0, 0)


def spread(block, axis, count):
    return exchange(jnp.broadcast_to(block[None], (count,) + block.shape), axis)


def partner(block):
    return lax.ppermute(block, "c", SWAP)


def shift(block, axis, by):
    return lax.ppermute(block, axis, [(i, (i + by) % 4) for i in range(4)])


def hidden_kernel(seat, mine, left, right, far, own_cols, other_cols, out, held, weights):
    x, y, c = seat[0], seat[1], seat[2]
    rows, feats = mine.shape
    cols = own_cols.shape[0] // NY
    for k, block in enumerate((mine, left, right, far)):
        held[k, :rows] = block[...]
        held[k, rows:] = jnp.zeros((64 - rows, feats), bf16)
    blocks = held[...].reshape(NX * 64, feats)

    half = own_cols.shape[0]
    weights[:half], weights[half:] = own_cols[...], other_cols[...]
    both = lax.dot_general(weights[...], blocks, (((1,), (1,)), ((), ())), preferred_element_type=f32)
    own, other = both[:half], both[half:]
    first, second = jnp.where(c == 0, own, other), jnp.where(c == 0, other, own)
    beside = y + 1 - 2 * lax.rem(y, 2)
    for k, off in enumerate((0, 3, 1, 2)):
        both = jnp.concatenate([first[:, 64 * k : 64 * k + 64], second[:, 64 * k : 64 * k + 64]], axis=1)
        for j, at in enumerate((y, beside, 3 - y, 3 - beside)):
            out[lax.rem(x + off, NX), at] = both[j * cols : (j + 1) * cols].astype(bf16)


def partial_hidden(seat, blocks, own_cols, other_cols, cols):
    vmem = pl.BlockSpec(memory_space=pltpu.VMEM)
    return pl.pallas_call(
        hidden_kernel,
        out_shape=jax.ShapeDtypeStruct((NX, NY, cols, 128), bf16),
        in_specs=[pl.BlockSpec(memory_space=pltpu.SMEM)] + [vmem] * 6,
        out_specs=vmem,
        scratch_shapes=[pltpu.VMEM((NX, 64, blocks[0].shape[1]), bf16), pltpu.VMEM((2 * NY * cols, blocks[0].shape[1]), bf16)],
        cost_estimate=pl.CostEstimate(flops=330_000_000, bytes_accessed=3_400_000, transcendentals=0),
    )(seat, *blocks, own_cols, other_cols)


def centre_kernel(centres, own, received, out):
    wide = centres[...].astype(f32)
    cinv = lax.rsqrt(jnp.sum(wide * wide, axis=1, keepdims=True) + norm_eps)
    unit_centre = wide * cinv
    gunit = own[...] + received[...]
    out[...] = cinv * (gunit - unit_centre * jnp.sum(unit_centre * gunit, axis=1, keepdims=True))


def centre_gradient(centres, own, received):
    rows, emb = centres.shape
    block = pl.BlockSpec(memory_space=pltpu.VMEM)
    return pl.pallas_call(
        centre_kernel,
        out_shape=jax.ShapeDtypeStruct((rows, emb), f32),
        in_specs=[block] * 3,
        out_specs=block,
        cost_estimate=pl.CostEstimate(flops=3_000_000, bytes_accessed=3_700_000, transcendentals=512),
    )(centres, own, received)


def split_pair(value):
    high = lax.reduce_precision(value, 8, 7)
    return high.astype(bf16), (value - high).astype(bf16)


def step_of(features, proj_in, proj_out, centres, labels):
    rows, _ = features.shape
    cols = proj_in.shape[1]
    emb = proj_out.shape[1]
    cen = centres.shape[0]
    images = NX * NY * rows
    lanes = emb // 4
    zi, xi, yi, ci = (lax.axis_index(a) for a in ("z", "x", "y", "c"))

    from_left = shift(features, "x", 1)
    from_right = shift(features, "x", 3)
    own_cols = proj_in.T
    own_out = spread(lax.dynamic_slice_in_dim(proj_out, ci * (emb // 2) + lax.rem(yi, 2) * lanes, lanes, 1), "z", NZ)
    own_cols = jnp.concatenate([own_cols, lax.ppermute(own_cols, "y", NEAR)], axis=0)
    own_cols = jnp.concatenate([own_cols, lax.ppermute(own_cols, "y", [(0, 3), (3, 0), (1, 2), (2, 1)])], axis=0)
    from_far = shift(from_left, "x", 1)
    other_cols = partner(own_cols)
    seat = jnp.stack([xi, yi, ci]).astype(jnp.int32)
    part = partial_hidden(seat, (features, from_left, from_right, from_far), own_cols, other_cols, cols)
    part = exchange(part, "x").reshape(NZ, cols, 128)
    part, labels = lax.optimization_barrier((part, labels))
    all_labels = lax.dynamic_update_slice_in_dim(jnp.zeros(NY * rows, jnp.int32), labels, yi * rows, 0)
    all_labels = lax.psum(all_labels, "y")
    all_labels = lax.dynamic_update_slice_in_dim(jnp.zeros(images, jnp.int32), all_labels, xi * NY * rows, 0)
    all_labels = lax.psum(all_labels, "x")

    all_labels = all_labels.reshape(images, 1)
    wide = centres.astype(f32)
    cinv = lax.rsqrt(jnp.sum(wide * wide, axis=1) + norm_eps)
    unit_centre = wide * cinv[:, None]
    own_low = unit_centre.astype(bf16)
    low = jnp.concatenate([own_low, partner(own_low)], axis=0)
    chip = ((zi * NX + xi) * NY + yi) * NC
    step = jnp.arange(cen, dtype=jnp.int32)
    position = jnp.concatenate([(chip + ci) * cen + step, (chip + 1 - ci) * cen + step])
    target = all_labels == position[None, :]

    beside_out = lax.ppermute(own_out, "y", NEAR)
    even = lax.rem(yi, 2) == 0
    own_out = jnp.concatenate([jnp.where(even, own_out, beside_out), jnp.where(even, beside_out, own_out)], axis=2)
    other_out = partner(own_out)
    hidden = jnp.sum(exchange(part, "z").astype(f32), axis=0).astype(bf16)
    hidden = spread(hidden, "z", NZ).reshape(NZ * cols, 128)

    def over_rows(left, right):
        return lax.dot_general(left, right, (((0,), (0,)), ((), ())), preferred_element_type=f32)

    def embed_with(out_rows):
        left = over_rows(hidden[:, :rows], out_rows[:, :cols].reshape(NZ * cols, emb // 2))
        return left + over_rows(hidden[:, 64 : 64 + rows], out_rows[:, cols:].reshape(NZ * cols, emb // 2))

    own, other = embed_with(own_out), embed_with(other_out)
    embed = jnp.concatenate([jnp.where(ci == 0, own, other), jnp.where(ci == 0, other, own)], axis=1)
    inverse = lax.rsqrt(jnp.sum(embed * embed, axis=1) + norm_eps)
    unit = embed * inverse[:, None]
    units = spread(unit.astype(bf16), XY, NX * NY).reshape(images, emb)

    chosen = jnp.dot(target.astype(bf16), low, preferred_element_type=f32).astype(bf16)
    chosen, units = lax.optimization_barrier((chosen, units))
    chosen = exchange(chosen.reshape(NX * NY, rows, emb), XY)
    chosen = jnp.sum(chosen.astype(f32), axis=0)

    cos_m = jnp.cos(f32(margin_angle))
    sin_m = jnp.sin(f32(margin_angle))
    cosine = lax.dot_general(units, low, (((1,), (1,)), ((), ())), preferred_element_type=f32)
    inner = 1.0 - cosine * cosine
    sine = jnp.sqrt(jnp.maximum(inner, sine_floor))
    logit = jnp.where(target, scale_logit * (cosine * cos_m - sine * sin_m), scale_logit * cosine)
    exps = jnp.exp(logit)
    slope = cos_m + jnp.where(inner > sine_floor, sin_m * cosine / sine, 0.0)
    rest = jnp.where(target, 0.0, exps)
    rest_sum = jnp.sum(rest, axis=1)
    rest_cos = jnp.sum(rest * cosine, axis=1)
    hit = jnp.sum(jnp.where(target, exps, 0.0), axis=1)
    hit_slope = jnp.sum(jnp.where(target, slope, 0.0), axis=1)
    hit_turn = jnp.sum(jnp.where(target, slope * cosine, 0.0), axis=1)

    pull = jnp.dot(lax.optimization_barrier(rest.astype(bf16)), low, preferred_element_type=f32).astype(bf16).reshape(NX * NY, rows, emb)
    tall = images // 128
    totals = jnp.concatenate(split_pair((rest_sum + hit).reshape(tall, 128)), axis=0)
    totals = jnp.pad(totals, ((0, 16 - 2 * tall), (0, 0))).reshape(4, emb)
    totals = jnp.broadcast_to(totals[None], (NX * NY, 4, emb))
    owned = jnp.stack([rest_sum, hit, rest_cos, hit_slope, hit_turn]).reshape(5, NX * NY, rows)
    owned = jnp.pad(owned.transpose(1, 0, 2), ((0, 0), (0, 0), (0, 64 - rows)))
    owned = jnp.concatenate(split_pair(owned), axis=1).reshape(NX * NY, 640)
    owned = jnp.pad(owned, ((0, 0), (0, 4 * emb - 640))).reshape(NX * NY, 4, emb)
    pull = jnp.concatenate([pull, totals, owned], axis=1)
    pull = exchange(pull, XY)
    pull = jnp.sum(pull.astype(f32), axis=0)
    totals = pull[rows : rows + 4].reshape(16, 128)
    totals = totals[:tall] + totals[tall : 2 * tall]
    owned = pull[rows + 4 :].reshape(4 * emb)[:640].reshape(10, 64)
    owned = jnp.pad(owned[:5] + owned[5:], ((0, 0), (0, 64)))

    width = emb // NZ

    def by_column(block):
        block = block.astype(bf16).reshape(4, rows // 4, NZ, width)
        return block.transpose(2, 1, 0, 3).reshape(NZ, rows // 4, 4 * width)

    pull = pull[:rows]
    common = jnp.concatenate(split_pair(totals) + split_pair(owned), axis=0)
    common = jnp.broadcast_to(common[None], (NZ,) + common.shape)
    pack = jnp.concatenate([by_column(pull), by_column(chosen), common], axis=1)
    pack = exchange(pack, "z")
    pack = jnp.sum(pack.astype(f32), axis=0)

    def by_row(block):
        return block.reshape(rows // 4, 4, width).transpose(1, 0, 2).reshape(rows, width)

    quarter = rows // 4
    pull, chosen = by_row(pack[:quarter]), by_row(pack[quarter : 2 * quarter])
    common = pack[2 * quarter :]
    total = (common[:tall] + common[tall : 2 * tall]).reshape(images, 1)
    owned = common[2 * tall : 2 * tall + 5, :rows] + common[2 * tall + 5 :, :rows]
    own_rest, own_hit, own_cos, own_slope, own_turn = (owned[k] for k in range(5))

    cosine_t = lax.dot_general(low, units, (((1,), (1,)), ((), ())), preferred_element_type=f32)
    target_t = position[:, None] == all_labels.reshape(1, images)
    rest_t = jnp.where(target_t, 0.0, jnp.exp(scale_logit * cosine_t)).astype(bf16)
    joined = lax.optimization_barrier(jnp.concatenate([rest_t, target_t.astype(bf16)], axis=1))
    weight = scale_logit * hit_slope[:, None] * (hit[:, None] / total - 1.0)
    scaled = (units.astype(f32) * (scale_logit / total)).astype(bf16)
    aimed = (units.astype(f32) * weight).astype(bf16)
    scaled = lax.optimization_barrier(jnp.concatenate([scaled, aimed], axis=0))

    def gradient_of(part):
        return jnp.dot(joined[part], scaled, preferred_element_type=f32)

    received = partner(gradient_of(slice(cen, None)))
    centre_grad = centre_gradient(centres, gradient_of(slice(0, cen)), received)

    own_scale = scale_logit / (own_rest + own_hit)
    dunit = own_scale[:, None] * (pull - (own_rest * own_slope)[:, None] * chosen)
    along = own_scale * (own_cos - own_rest * own_turn)
    unit_cols = lax.dynamic_slice_in_dim(unit, zi * width, width, 1)
    emb_grad = inverse[:, None] * (dunit - unit_cols * along[:, None])
    return (centre_grad, emb_grad)


def solution(mesh):
    fine = Mesh(np.asarray(mesh.devices).reshape(NZ, NX, NY, NC), ("z", "x", "y", "c"))
    img = ("x", "y", "c")
    every = ("z", "x", "y", "c")
    return jax.shard_map(
        step_of,
        mesh=fine,
        in_specs=(P(img, "z"), P("z", img), P("z", None), P(every, None), P(img)),
        out_specs=(P(every, None), P(img, "z")),
        check_vma=False,
    )
```

```python
import jax
import jax.numpy as jnp
import numpy as np
from jax import lax
from jax.experimental import pallas as pl
from jax.experimental.pallas import tpu as pltpu
from jax.sharding import Mesh, PartitionSpec as P


norm_eps = 1e-06
scale_logit = 64.0
margin_angle = 0.5
sine_floor = 0.04

NZ, NX, NY, NC = 16, 4, 4, 2
XY = ("x", "y")
SWAP = [(0, 1), (1, 0)]
f32 = jnp.float32
bf16 = jnp.bfloat16


def exchange(blocks, axis):
    return lax.all_to_all(blocks, axis, 0, 0)


def spread(block, axis, count):
    return exchange(jnp.broadcast_to(block[None], (count,) + block.shape), axis)


def partner(block):
    return lax.ppermute(block, "c", SWAP)


def shift(block, axis, by):
    return lax.ppermute(block, axis, [(i, (i + by) % 4) for i in range(4)])


def hidden_kernel(seat, mine, left, right, far, own_cols, other_cols, out, held, weights):
    x, y, c = seat[0], seat[1], seat[2]
    rows, feats = mine.shape
    cols = own_cols.shape[0] // NY
    for k, block in enumerate((mine, left, right, far)):
        held[k, :rows] = block[...]
        held[k, rows:] = jnp.zeros((64 - rows, feats), bf16)
    blocks = held[...].reshape(NX * 64, feats)

    half = own_cols.shape[0]
    weights[:half], weights[half:] = own_cols[...], other_cols[...]
    both = lax.dot_general(weights[...], blocks, (((1,), (1,)), ((), ())), preferred_element_type=f32)
    own, other = both[:half], both[half:]
    first, second = jnp.where(c == 0, own, other), jnp.where(c == 0, other, own)
    beside = y + 1 - 2 * lax.rem(y, 2)
    for k, off in enumerate((0, 3, 1, 2)):
        both = jnp.concatenate([first[:, 64 * k : 64 * k + 64], second[:, 64 * k : 64 * k + 64]], axis=1)
        for j, at in enumerate((y, beside, 3 - y, 3 - beside)):
            out[lax.rem(x + off, NX), at] = both[j * cols : (j + 1) * cols].astype(bf16)


def partial_hidden(seat, blocks, own_cols, other_cols, cols):
    vmem = pl.BlockSpec(memory_space=pltpu.VMEM)
    return pl.pallas_call(
        hidden_kernel,
        out_shape=jax.ShapeDtypeStruct((NX, NY, cols, 128), bf16),
        in_specs=[pl.BlockSpec(memory_space=pltpu.SMEM)] + [vmem] * 6,
        out_specs=vmem,
        scratch_shapes=[pltpu.VMEM((NX, 64, blocks[0].shape[1]), bf16), pltpu.VMEM((2 * NY * cols, blocks[0].shape[1]), bf16)],
        cost_estimate=pl.CostEstimate(flops=330_000_000, bytes_accessed=3_400_000, transcendentals=0),
    )(seat, *blocks, own_cols, other_cols)


def centre_kernel(centres, own, received, out):
    wide = centres[...].astype(f32)
    cinv = lax.rsqrt(jnp.sum(wide * wide, axis=1, keepdims=True) + norm_eps)
    unit_centre = wide * cinv
    gunit = own[...] + received[...]
    out[...] = cinv * (gunit - unit_centre * jnp.sum(unit_centre * gunit, axis=1, keepdims=True))


def centre_gradient(centres, own, received):
    rows, emb = centres.shape
    block = pl.BlockSpec(memory_space=pltpu.VMEM)
    return pl.pallas_call(
        centre_kernel,
        out_shape=jax.ShapeDtypeStruct((rows, emb), f32),
        in_specs=[block] * 3,
        out_specs=block,
        cost_estimate=pl.CostEstimate(flops=3_000_000, bytes_accessed=3_700_000, transcendentals=512),
    )(centres, own, received)


def split_pair(value):
    high = lax.reduce_precision(value, 8, 7)
    return high.astype(bf16), (value - high).astype(bf16)


def step_of(features, proj_in, proj_out, centres, labels):
    rows, _ = features.shape
    cols = proj_in.shape[1]
    emb = proj_out.shape[1]
    cen = centres.shape[0]
    images = NX * NY * rows
    zi, xi, yi, ci = (lax.axis_index(a) for a in ("z", "x", "y", "c"))

    from_left = shift(features, "x", 1)
    from_right = shift(features, "x", 3)
    own_cols = proj_in.T
    own_out = spread(lax.dynamic_slice_in_dim(proj_out, ci * (emb // 2), emb // 2, 1), "z", NZ)
    own_cols = jnp.concatenate([own_cols, lax.ppermute(own_cols, "y", [(0, 1), (1, 0), (2, 3), (3, 2)])], axis=0)
    own_cols = jnp.concatenate([own_cols, lax.ppermute(own_cols, "y", [(0, 3), (3, 0), (1, 2), (2, 1)])], axis=0)
    from_far = shift(from_left, "x", 1)
    other_cols = partner(own_cols)
    seat = jnp.stack([xi, yi, ci]).astype(jnp.int32)
    part = partial_hidden(seat, (features, from_left, from_right, from_far), own_cols, other_cols, cols)
    all_labels = lax.dynamic_update_slice_in_dim(jnp.zeros(NY * rows, jnp.int32), labels, yi * rows, 0)
    all_labels = lax.psum(all_labels, "y")
    all_labels = lax.dynamic_update_slice_in_dim(jnp.zeros(images, jnp.int32), all_labels, xi * NY * rows, 0)
    all_labels = lax.psum(all_labels, "x")
    part = exchange(part, "x").reshape(NZ, cols, 128)

    all_labels = all_labels.reshape(images, 1)
    wide = centres.astype(f32)
    cinv = lax.rsqrt(jnp.sum(wide * wide, axis=1) + norm_eps)
    unit_centre = wide * cinv[:, None]
    own_low = unit_centre.astype(bf16)
    low = jnp.concatenate([own_low, partner(own_low)], axis=0)
    chip = ((zi * NX + xi) * NY + yi) * NC
    step = jnp.arange(cen, dtype=jnp.int32)
    position = jnp.concatenate([(chip + ci) * cen + step, (chip + 1 - ci) * cen + step])
    target = all_labels == position[None, :]

    other_out = partner(own_out)
    hidden = jnp.sum(exchange(part, "z").astype(f32), axis=0).astype(bf16)
    hidden = spread(hidden, "z", NZ).reshape(NZ * cols, 128)

    def over_rows(left, right):
        return lax.dot_general(left, right, (((0,), (0,)), ((), ())), preferred_element_type=f32)

    def embed_with(out_rows):
        left = over_rows(hidden[:, :rows], out_rows[:, :cols].reshape(NZ * cols, emb // 2))
        return left + over_rows(hidden[:, 64 : 64 + rows], out_rows[:, cols:].reshape(NZ * cols, emb // 2))

    own, other = embed_with(own_out), embed_with(other_out)
    embed = jnp.concatenate([jnp.where(ci == 0, own, other), jnp.where(ci == 0, other, own)], axis=1)
    inverse = lax.rsqrt(jnp.sum(embed * embed, axis=1) + norm_eps)
    unit = embed * inverse[:, None]
    units = spread(unit.astype(bf16), XY, NX * NY).reshape(images, emb)

    chosen = jnp.dot(target.astype(bf16), low, preferred_element_type=f32).astype(bf16)
    chosen, units = lax.optimization_barrier((chosen, units))
    chosen = exchange(chosen.reshape(NX * NY, rows, emb), XY)
    chosen = jnp.sum(chosen.astype(f32), axis=0)

    cos_m = jnp.cos(f32(margin_angle))
    sin_m = jnp.sin(f32(margin_angle))
    cosine = lax.dot_general(units, low, (((1,), (1,)), ((), ())), preferred_element_type=f32)
    inner = 1.0 - cosine * cosine
    sine = jnp.sqrt(jnp.maximum(inner, sine_floor))
    logit = jnp.where(target, scale_logit * (cosine * cos_m - sine * sin_m), scale_logit * cosine)
    exps = jnp.exp(logit)
    slope = cos_m + jnp.where(inner > sine_floor, sin_m * cosine / sine, 0.0)
    rest = jnp.where(target, 0.0, exps)
    rest_sum = jnp.sum(rest, axis=1)
    rest_cos = jnp.sum(rest * cosine, axis=1)
    hit = jnp.sum(jnp.where(target, exps, 0.0), axis=1)
    hit_slope = jnp.sum(jnp.where(target, slope, 0.0), axis=1)
    hit_turn = jnp.sum(jnp.where(target, slope * cosine, 0.0), axis=1)

    pull = jnp.dot(lax.optimization_barrier(rest.astype(bf16)), low, preferred_element_type=f32).astype(bf16).reshape(NX * NY, rows, emb)
    tall = images // 128
    totals = jnp.concatenate(split_pair((rest_sum + hit).reshape(tall, 128)), axis=0)
    totals = jnp.pad(totals, ((0, 16 - 2 * tall), (0, 0))).reshape(4, emb)
    totals = jnp.broadcast_to(totals[None], (NX * NY, 4, emb))
    owned = jnp.stack([rest_sum, hit, rest_cos, hit_slope, hit_turn]).reshape(5, NX * NY, rows)
    owned = jnp.pad(owned.transpose(1, 0, 2), ((0, 0), (0, 0), (0, 64 - rows)))
    owned = jnp.concatenate(split_pair(owned), axis=1).reshape(NX * NY, 640)
    owned = jnp.pad(owned, ((0, 0), (0, 4 * emb - 640))).reshape(NX * NY, 4, emb)
    pull = jnp.concatenate([pull, totals, owned], axis=1)
    pull = exchange(pull, XY)
    pull = jnp.sum(pull.astype(f32), axis=0)
    totals = pull[rows : rows + 4].reshape(16, 128)
    totals = totals[:tall] + totals[tall : 2 * tall]
    owned = pull[rows + 4 :].reshape(4 * emb)[:640].reshape(10, 64)
    owned = jnp.pad(owned[:5] + owned[5:], ((0, 0), (0, 64)))

    width = emb // NZ

    def by_column(block):
        block = block.astype(bf16).reshape(4, rows // 4, NZ, width)
        return block.transpose(2, 1, 0, 3).reshape(NZ, rows // 4, 4 * width)

    pull = pull[:rows]
    common = jnp.concatenate(split_pair(totals) + split_pair(owned), axis=0)
    common = jnp.broadcast_to(common[None], (NZ,) + common.shape)
    pack = jnp.concatenate([by_column(pull), by_column(chosen), common], axis=1)
    pack = exchange(pack, "z")
    pack = jnp.sum(pack.astype(f32), axis=0)

    def by_row(block):
        return block.reshape(rows // 4, 4, width).transpose(1, 0, 2).reshape(rows, width)

    quarter = rows // 4
    pull, chosen = by_row(pack[:quarter]), by_row(pack[quarter : 2 * quarter])
    common = pack[2 * quarter :]
    total = (common[:tall] + common[tall : 2 * tall]).reshape(images, 1)
    owned = common[2 * tall : 2 * tall + 5, :rows] + common[2 * tall + 5 :, :rows]
    own_rest, own_hit, own_cos, own_slope, own_turn = (owned[k] for k in range(5))

    cosine_t = lax.dot_general(low, units, (((1,), (1,)), ((), ())), preferred_element_type=f32)
    target_t = position[:, None] == all_labels.reshape(1, images)
    rest_t = jnp.where(target_t, 0.0, jnp.exp(scale_logit * cosine_t)).astype(bf16)
    joined = lax.optimization_barrier(jnp.concatenate([rest_t, target_t.astype(bf16)], axis=1))
    weight = scale_logit * hit_slope[:, None] * (hit[:, None] / total - 1.0)
    scaled = (units.astype(f32) * (scale_logit / total)).astype(bf16)
    aimed = (units.astype(f32) * weight).astype(bf16)
    scaled = lax.optimization_barrier(jnp.concatenate([scaled, aimed], axis=0))

    def gradient_of(part):
        return jnp.dot(joined[part], scaled, preferred_element_type=f32)

    received = partner(gradient_of(slice(cen, None)))
    centre_grad = centre_gradient(centres, gradient_of(slice(0, cen)), received)

    own_scale = scale_logit / (own_rest + own_hit)
    dunit = own_scale[:, None] * (pull - (own_rest * own_slope)[:, None] * chosen)
    along = own_scale * (own_cos - own_rest * own_turn)
    unit_cols = lax.dynamic_slice_in_dim(unit, zi * width, width, 1)
    emb_grad = inverse[:, None] * (dunit - unit_cols * along[:, None])
    return (centre_grad, emb_grad)


def solution(mesh):
    fine = Mesh(np.asarray(mesh.devices).reshape(NZ, NX, NY, NC), ("z", "x", "y", "c"))
    img = ("x", "y", "c")
    every = ("z", "x", "y", "c")
    return jax.shard_map(
        step_of,
        mesh=fine,
        in_specs=(P(img, "z"), P("z", img), P("z", None), P(every, None), P(img)),
        out_specs=(P(every, None), P(img, "z")),
        check_vma=False,
    )
```
